256 devices in a mesh: section: 2 (over core), row: 32 (over z, y), col: 4 (over x).
Axes of the slice: x: 4, y: 4, z: 8, core: 2. Of those that a mesh axis runs over, the one named last changes fastest.
Arguments:
- hidden_in: bfloat16 [32, 256, 3072], P('row', None, 'col')
- patch_ends: int32 [32, 4], P('row'), may hold values from 1 to 256, as said below
- timestep: int32 [32], P('row'), may hold values from 0 to 999
- mod_weight: bfloat16 [2, 256, 3, 3072], P('section'), may hold values from -0.75 to 0.75
- qkv_weight: bfloat16 [2, 3072, 3, 3072], P('section', 'row', None, 'col'), may hold values from -0.109375 to 0.109375
- out_weight: bfloat16 [2, 3072, 3072], P('section', 'col', 'row'), may hold values from -0.109375 to 0.109375
- stale_keys: bfloat16 [2, 32, 256, 3072], P('section', 'row', None, 'col'), may hold values from -1.5 to 1.5
- stale_values: bfloat16 [2, 32, 256, 3072], P('section', 'row', None, 'col'), may hold values from -6 to 6
Outputs:
- layer_out: bfloat16 [2, 32, 256, 3072], P('section', 'row', None, 'col')
The draws below stay inside these ranges and needn't reach their ends.
Inputs may be any that keep to these rules, and one draw needn't show every extreme that they name: patch_ends rises along each request's 4 patches; each patch holds at least one and at most 64 positions, and in every draw some request has all 4 patches of exactly 64 positions.
All inputs are finite; a program needn't handle non-finite values.
Results may differ from the reference program's by a relative error of at most 0.018.
Values may be sent and summed in bfloat16 or wider, within the bound.
A program may use at most 128 MiB of HBM per device.

```python
import math
import jax
import jax.numpy as jnp
from jax import lax

D = 3072
HD = 128
FREQ = 256
NP = 4
PATCH = 64
REQ = 32
SLOT = 256
LAYERS = 2


def draw_hidden_in(key, part):
    key_base = jax.random.fold_in(key, 11)
    key_cols = jax.random.fold_in(key, 12)
    key_rows = jax.random.fold_in(key, 13)
    feat_pos = jnp.arange(D, dtype=jnp.float32)[None, None, :] / D - 0.5
    rough = jnp.exp(jax.random.uniform(key_cols, (1, 1, D), jnp.float32, jnp.log(0.7), jnp.log(1.4)))
    row_scale = jnp.exp(jax.random.uniform(key_rows, (REQ, SLOT, 1), jnp.float32, jnp.log(0.5), jnp.log(2.0)))
    col_scale = jnp.exp(jnp.log(6.0) * feat_pos) * rough
    base_vals = jax.random.truncated_normal(key_base, -4.0, 4.0, (REQ, SLOT, D), jnp.float32)
    return (0.5 * base_vals * col_scale * row_scale).astype(jnp.bfloat16)


def draw_patch_ends(key, part):
    key_sizes = jax.random.fold_in(key, 21)
    key_pick = jax.random.fold_in(key, 22)
    sizes = jax.random.randint(key_sizes, (REQ, NP), PATCH // 4, PATCH + 1)
    chosen = jax.random.randint(key_pick, (), 0, REQ)
    full_row = (jnp.arange(REQ)[:, None] == chosen) & (jnp.arange(NP)[None, :] >= 0)
    sizes = jnp.where(full_row, PATCH, sizes)
    return jnp.cumsum(sizes, axis=1).astype(jnp.int32)


def touch_ends(entries, rng, low, top_value):
    spot = [jax.random.randint(jax.random.fold_in(rng, axis), (), 0, length) for axis, length in enumerate(entries.shape)]
    widest = entries.shape.index(max(entries.shape))
    beside = spot[:widest] + [(spot[widest] + 1) % entries.shape[widest]] + spot[widest + 1:]
    return entries.at[tuple(spot)].set(low).at[tuple(beside)].set(top_value)


def block_levels(rng, dims, shards, low, high):
    level, own = 1.0, jax.random.fold_in(rng, 6)
    for position, shards_of in shards:
        steps = jnp.exp(jax.random.uniform(jax.random.fold_in(own, position), (shards_of,), jnp.float32, low / len(shards), high / len(shards)))
        level = level * jnp.repeat(steps, dims[position] // shards_of).reshape([-1 if axis == position else 1 for axis in range(len(dims))])
    return level


def centred(stream_key, shape, width, reach, pieces=(), kind=jnp.bfloat16):
    gain = block_levels(stream_key, shape, pieces, -0.22, 0.18) if pieces else 1.0
    entries = jax.random.normal(stream_key, shape, jnp.float32) * width * gain
    return jnp.minimum(jnp.maximum(entries, -reach), reach).astype(kind)


def setup_inputs(seed: int = 0) -> dict:
    key_list = jax.random.split(jax.random.key(seed), 9)
    return {
        "hidden_in": draw_hidden_in(jax.random.fold_in(key_list[8], 71), 0),
        "patch_ends": draw_patch_ends(jax.random.fold_in(key_list[8], 71), 0),
        "timestep": touch_ends(jax.random.randint(key_list[2], (REQ,), 0, 1000), jax.random.fold_in(key_list[2], 1), 0, 999).astype(jnp.int32),
        "mod_weight": centred(key_list[3], (LAYERS, FREQ, 3, D), 0.125, 0.75, ((0, 2),)),
        "qkv_weight": centred(key_list[4], (LAYERS, D, 3, D), D ** -0.5, 0.109375, ((0, 2), (1, 32), (3, 4))),
        "out_weight": centred(key_list[5], (LAYERS, D, D), D ** -0.5, 0.109375, ((0, 2), (1, 4), (2, 32))),
        "stale_keys": jnp.clip(jax.random.uniform(key_list[6], (LAYERS, REQ, SLOT, D), jnp.float32, -1.5, 1.5) * block_levels(key_list[6], (LAYERS, REQ, SLOT, D), ((0, 2), (1, 32), (3, 4)), -0.4, 0.0), -1.5, 1.5).astype(jnp.bfloat16),
        "stale_values": centred(key_list[7], (LAYERS, REQ, SLOT, D), 1.0, 6.0, ((0, 2), (1, 32), (3, 4))),
    }


def embed_time(timestep, feat_width):
    half_width = feat_width // 2
    frequency = jnp.exp(jnp.arange(half_width, dtype=jnp.float32) * (-math.log(10000.0) / half_width))
    angles = timestep.astype(jnp.float32)[:, None] * frequency[None, :]
    return jnp.concatenate([jnp.cos(angles), jnp.sin(angles)], axis=1).astype(jnp.bfloat16)

def head_norm(raw_proj):
    shaped = raw_proj.reshape(raw_proj.shape[:-1] + (raw_proj.shape[-1] // HD, HD))
    scaled = shaped / jnp.sqrt(lax.optimization_barrier(jnp.mean(shaped * shaped, axis=-1, keepdims=True)) + 1e-06)
    return scaled.reshape(raw_proj.shape).astype(jnp.bfloat16)

def attend(queries, key_rows, value_rows, key_ok):
    query_heads = queries.astype(jnp.float32).reshape(queries.shape[0], -1, HD)
    key_heads = key_rows.astype(jnp.float32).reshape(key_rows.shape[0], -1, HD)
    value_heads = value_rows.astype(jnp.float32).reshape(value_rows.shape[0], -1, HD)
    scores = jnp.einsum('qhd,khd->hqk', query_heads, key_heads) / math.sqrt(HD)
    weights = jnp.exp(scores) * key_ok[None, None, :]
    weights = (weights / lax.optimization_barrier(jnp.sum(weights, axis=-1, keepdims=True))).astype(jnp.bfloat16)
    mixed = jnp.einsum('hqk,khd->qhd', weights.astype(jnp.float32), value_heads)
    return mixed.reshape(queries.shape).astype(jnp.bfloat16)

def reference(hidden_in, patch_ends, timestep, mod_weight, qkv_weight, out_weight, stale_keys, stale_values):
    time_feats = embed_time(timestep, FREQ)
    positions = jnp.arange(SLOT, dtype=jnp.int32)
    seq_len = patch_ends[:, NP - 1]
    valid = (positions[None, :] < seq_len[:, None])[:, :, None]
    key_ok = (positions[None, :] < seq_len[:, None]).astype(jnp.float32)
    patch_starts = jnp.concatenate([jnp.zeros((REQ, 1), jnp.int32), patch_ends[:, :NP - 1].astype(jnp.int32)], axis=1)
    layer_input = hidden_in
    results = []
    for layer_index in range(LAYERS):
        modulation = jnp.dot(time_feats, mod_weight[layer_index].reshape(FREQ, 3 * D), preferred_element_type=jnp.float32).reshape(REQ, 3, D)
        shift_vec = modulation[:, 0]
        scale_vec = modulation[:, 1]
        gate_vec = modulation[:, 2]
        as_float = layer_input.astype(jnp.float32)
        row_mean = lax.optimization_barrier(jnp.mean(as_float, axis=-1, keepdims=True))
        row_var = lax.optimization_barrier(jnp.mean(as_float * as_float, axis=-1, keepdims=True)) - row_mean * row_mean
        normed = (as_float - row_mean) / jnp.sqrt(row_var + 1e-06)
        modulated = (normed * (1.0 + scale_vec[:, None, :]) + shift_vec[:, None, :]).astype(jnp.bfloat16)
        projected = jnp.dot(modulated.reshape(REQ * SLOT, D), qkv_weight[layer_index].reshape(D, 3 * D), preferred_element_type=jnp.float32).reshape(REQ, SLOT, 3, D)
        queries = head_norm(projected[:, :, 0])
        fresh_keys = head_norm(projected[:, :, 1])
        fresh_values = projected[:, :, 2].astype(jnp.bfloat16)

        def one_request(items):
            query_rows, keys_new, values_new, keys_old, values_old, ends_row, starts_row, ok_row = items
            totals = jnp.zeros(query_rows.shape, jnp.bfloat16)
            for patch_index in range(NP):
                is_fresh = (positions < ends_row[patch_index])[:, None]
                mixed = attend(query_rows, jnp.where(is_fresh, keys_new, keys_old), jnp.where(is_fresh, values_new, values_old), ok_row)
                row_mask = ((positions >= starts_row[patch_index]) & (positions < ends_row[patch_index]))[:, None]
                totals = jnp.where(row_mask, mixed, totals)
            return totals
        attended = lax.map(one_request, (queries, fresh_keys, fresh_values, stale_keys[layer_index], stale_values[layer_index], patch_ends, patch_starts, key_ok))
        branch = jnp.dot(attended.reshape(REQ * SLOT, D), out_weight[layer_index], preferred_element_type=jnp.float32).reshape(REQ, SLOT, D)
        updated = as_float + gate_vec[:, None, :] * branch
        layer_result = jnp.where(valid, updated, 0.0).astype(jnp.bfloat16)
        results.append(layer_result)
        layer_input = layer_result
    return jnp.stack(results)
```

```python
import functools
import math

import jax
import jax.numpy as jnp
from jax import lax
from jax.experimental import pallas as pl
from jax.experimental.pallas import tpu as pltpu
from jax.sharding import PartitionSpec as P

HD = 128
FREQ = 256
NX, NY, NZ = 4, 4, 8
KB = 96
CW = 768
SUP = NY * KB
SLOT = 256
HEADS = CW // HD
OA = 512
OB = CW - OA
MESH = pl.DeviceIdType.MESH
F32 = jnp.float32
BF16 = jnp.bfloat16
N_SEM = 128


def embed_time(timestep):
    half_width = FREQ // 2
    frequency = jnp.exp(
        jnp.arange(half_width, dtype=F32) * (-math.log(10000.0) / half_width)
    )
    angles = timestep.astype(F32)[:, None] * frequency[None, :]
    return jnp.concatenate([jnp.cos(angles), jnp.sin(angles)], axis=1).astype(BF16)


class Links:
    def __init__(self, send_sem, recv_sem):
        self.send_sem, self.recv_sem = send_sem, recv_sem
        self.count = 0
        self.started = []

    def slot(self):
        self.count += 1
        return self.count - 1

    def copy(self, index, source, target, device):
        return pltpu.make_async_remote_copy(
            src_ref=source, dst_ref=target, send_sem=self.send_sem.at[index],
            recv_sem=self.recv_sem.at[index], device_id=device, device_id_type=MESH,
        )

    def start(self, out_view, in_view, device, target=None):
        index = self.slot()
        outgoing = self.copy(index, out_view, out_view if target is None else target, device)
        outgoing.start()
        self.started.append(outgoing)
        return self.copy(index, in_view, in_view, device)


class Gather:
    def __init__(self, links, pos, devs, views):
        self.links, self.devs = links, devs
        self.y, self.z = pos
        self.a_shard, self.a_half, self.a_sup, self.b_shard, self.b_half = views
        self.inc = {}

    def zi(self, off):
        return lax.rem(self.z + (off + NZ), NZ)

    def yi(self, off):
        return lax.rem(self.y + (off + NY), NY)

    def go(self, key, out_view, in_view, device):
        self.inc[key] = self.links.start(out_view, in_view, self.devs[device])

    def wait(self, *key):
        self.inc.pop(key).wait_recv()

    def ya_own(self):
        for sign, dev in ((1, "y+"), (-1, "y-")):
            self.go(("ya", sign), self.a_shard(self.z, self.y), self.a_shard(self.z, self.yi(-sign)), dev)

    def ya_relay(self):
        for sign, dev, half in ((1, "y+", 0), (-1, "y-", 1)):
            self.wait("ya", sign)
            self.go(("yah", sign), self.a_half(self.z, self.yi(-sign), half), self.a_half(self.z, self.yi(-2 * sign), half), dev)

    def ya_fin(self):
        for sign in (1, -1):
            self.wait("yah", sign)

    def zb_send(self, d):
        for sign, dev, half in ((1, "z+", 0), (-1, "z-", 1)):
            if d > 0:
                self.wait("zb", sign, d - 1)
            here, there = self.zi(-sign * d), self.zi(-sign * (d + 1))
            if d < NZ // 2 - 1:
                self.go(("zb", sign, d), self.b_shard(here, self.y), self.b_shard(there, self.y), dev)
            else:
                self.go(("zb", sign, d), self.b_half(here, self.y, half), self.b_half(there, self.y, half), dev)

    def zb_fin(self):
        for sign in (1, -1):
            self.wait("zb", sign, NZ // 2 - 1)

    def yb_own(self, off):
        for sign, dev in ((1, "y+"), (-1, "y-")):
            self.go(("yb", off, sign), self.b_shard(self.zi(off), self.y), self.b_shard(self.zi(off), self.yi(-sign)), dev)

    def yb_relay(self, off):
        for sign, dev, half in ((1, "y+", 0), (-1, "y-", 1)):
            self.wait("yb", off, sign)
            self.go(("ybh", off, sign), self.b_half(self.zi(off), self.yi(-sign), half), self.b_half(self.zi(off), self.yi(-2 * sign), half), dev)

    def yb_fin(self, off):
        for sign in (1, -1):
            self.wait("ybh", off, sign)

    def za_send(self, d, half):
        for sign, dev in ((1, "z+"), (-1, "z-")):
            if d == NZ // 2 - 1 and (half == 0) != (sign == 1):
                continue
            if d > 0:
                self.wait("za", sign, d - 1, half)
            here, there = self.zi(-sign * d), self.zi(-sign * (d + 1))
            self.go(("za", sign, d, half), self.a_sup(here, half), self.a_sup(there, half), dev)

    def za_fin(self):
        last = NZ // 2 - 1
        for sign, half in ((1, 1), (-1, 0)):
            self.wait("za", sign, last - 1, half)
        for sign, half in ((1, 0), (-1, 1)):
            self.wait("za", sign, last, half)


def nt_dot(left, right):
    return lax.dot_general(left, right, (((1,), (1,)), ((), ())), preferred_element_type=F32)


def kernel(
    ends_ref, feats_ref, hidden_hbm, mod_hbm, qkv_hbm, out_hbm, keys_hbm, values_hbm,
    result_ref,
    wbuf, woa, wob, modw, modv, xbuf, xm, acc, stk, stv, att, part, own_part, rs_in, res,
    send_sem, recv_sem, local_sem, gate_sem,
):
    s = lax.axis_index("section")
    row = lax.axis_index("row")
    x = lax.axis_index("col")
    z, y = row // NY, lax.rem(row, NY)

    def zy(zz, yy):
        return lax.rem(zz + NZ, NZ) * NY + lax.rem(yy + NY, NY)

    def xi(off):
        return lax.rem(x + (off + NX), NX)

    devs = {
        "y+": (s, zy(z, y + 1), x), "y-": (s, zy(z, y - 1), x),
        "z+": (s, zy(z + 1, y), x), "z-": (s, zy(z - 1, y), x),
        "x+": (s, row, xi(1)), "x-": (s, row, xi(-1)),
        "mate": (1 - s, row, x),
    }
    local = [
        pltpu.make_async_copy(qkv_hbm, wbuf.at[:, z, y], local_sem.at[0]),
        pltpu.make_async_copy(out_hbm.at[:, pl.ds(0, OA)], woa.at[z, y], local_sem.at[1]),
        pltpu.make_async_copy(out_hbm.at[:, pl.ds(OA, OB)], wob.at[z, y], local_sem.at[2]),
        pltpu.make_async_copy(mod_hbm, modw, local_sem.at[3]),
        pltpu.make_async_copy(keys_hbm, stk, local_sem.at[4]),
        pltpu.make_async_copy(values_hbm, stv, local_sem.at[5]),
    ]
    for copy in local:
        copy.start()
    load_x = pltpu.make_async_copy(hidden_hbm, xbuf.at[x], local_sem.at[6])

    @pl.when(s == 0)
    def _():
        load_x.start()

    barrier = pltpu.get_barrier_semaphore()
    for device in devs.values():
        pl.semaphore_signal(barrier, inc=1, device_id=device, device_id_type=MESH)
    pl.semaphore_wait(barrier, len(devs))

    links = Links(send_sem, recv_sem)
    qkv = Gather(links, (y, z), devs, (
        lambda zz, yy: wbuf.at[0, zz, yy],
        lambda zz, yy, h: wbuf.at[0, zz, yy, pl.ds(h * (KB // 2), KB // 2)],
        lambda zz, h: wbuf.at[0, zz, pl.ds(2 * h, 2)],
        lambda zz, yy: wbuf.at[pl.ds(1, 2), zz, yy],
        lambda zz, yy, h: wbuf.at[1 + h, zz, yy],
    ))
    out = Gather(links, (y, z), devs, (
        lambda zz, yy: woa.at[zz, yy],
        lambda zz, yy, h: woa.at[zz, yy, pl.ds(h * (KB // 2), KB // 2)],
        lambda zz, h: woa.at[zz, pl.ds(2 * h, 2)],
        lambda zz, yy: wob.at[zz, yy],
        lambda zz, yy, h: wob.at[zz, yy, pl.ds(h * (KB // 2), KB // 2)],
    ))

    handed = links.slot()
    inc = {}

    def x_start():
        @pl.when(s == 0)
        def _():
            load_x.wait()

        @pl.when(s == 1)
        def _():
            links.copy(handed, res, xbuf.at[x], devs["mate"]).wait_recv()

        for sign, dev in ((1, "x+"), (-1, "x-")):
            inc["x", sign] = links.start(xbuf.at[x], xbuf.at[xi(-sign)], devs[dev])

    def x_relay():
        half_rows = SLOT // 2
        for sign, dev, half in ((1, "x+", 0), (-1, "x-", 1)):
            rows = pl.ds(half * half_rows, half_rows)
            inc["x", sign].wait_recv()
            inc["xh", sign] = links.start(xbuf.at[xi(-sign), rows], xbuf.at[xi(-2 * sign), rows], devs[dev])

    def x_fin():
        for sign in (1, -1):
            inc["xh", sign].wait_recv()

    def modulation():
        local[3].wait()

        def body(j, _):
            modv[j] = jnp.dot(feats_ref[...], modw[j], preferred_element_type=F32)
            return 0

        lax.fori_loop(0, 3, body, 0)

    def layer_norm():
        width = NX * CW

        def body(i, _):
            rows = pl.ds(pl.multiple_of(i * 16, 16), 16)
            parts = [xbuf[c, rows, :].astype(F32) for c in range(NX)]
            total = sum(jnp.sum(p, axis=-1, keepdims=True) for p in parts)
            squares = sum(jnp.sum(p * p, axis=-1, keepdims=True) for p in parts)
            mean = total / width
            var = squares / width - mean * mean
            inv = 1.0 / jnp.sqrt(var + 1e-06)
            for b in range(NZ):
                lanes = pl.ds(b * SUP, SUP)
                piece = parts[b // 2][:, (b % 2) * SUP:(b % 2 + 1) * SUP]
                normed = (piece - mean) * inv
                xm[b, rows, :] = (normed * (1.0 + modv[1, 0:1, lanes]) + modv[0, 0:1, lanes]).astype(BF16)
            return 0

        lax.fori_loop(0, SLOT // 16, body, 0)

    def project(offs, first):
        def body(t, _):
            j = t // 3
            lanes = pl.ds(pl.multiple_of(lax.rem(t, 3) * 256, 256), 256)
            total = None
            for off in offs:
                zz = qkv.zi(off)
                block = wbuf[j, zz, :, :, lanes].reshape(SUP, 256)
                term = jnp.dot(xm[zz], block, preferred_element_type=F32)
                total = term if total is None else total + term
            if first:
                acc[j, :, lanes] = total
            else:
                acc[j, :, lanes] += total
            return 0

        lax.fori_loop(0, 9, body, 0)

    e0, e1, e2, e3 = (ends_ref[0, m] for m in range(4))
    q_pos = lax.broadcasted_iota(jnp.int32, (SLOT, 1), 0)
    limit = jnp.where(q_pos < e0, e0, jnp.where(q_pos < e1, e1, jnp.where(q_pos < e2, e2, e3)))

    def attend(first_head, heads):
        def body(h, _):
            lanes = pl.ds(pl.multiple_of(h * HD, HD), HD)
            k_pos = lax.broadcasted_iota(jnp.int32, (SLOT, SLOT), 1)
            fresh = k_pos < limit
            ok = k_pos < e3

            def norm(raw):
                return (raw * (1.0 / jnp.sqrt(jnp.mean(raw * raw, axis=-1, keepdims=True) + 1e-06))).astype(BF16)

            q = norm(acc[0, :, lanes])
            k = norm(acc[1, :, lanes])
            v = acc[2, :, lanes].astype(BF16)
            scores = jnp.where(fresh, nt_dot(q, k), nt_dot(q, stk[:, lanes])) * (1.0 / math.sqrt(HD))
            weights = jnp.where(ok, jnp.exp(scores), 0.0)
            weights = weights * (1.0 / jnp.sum(weights, axis=-1, keepdims=True))
            new_part = jnp.where(fresh, weights, 0.0).astype(BF16)
            old_part = jnp.where(fresh, 0.0, weights).astype(BF16)
            mixed = jnp.dot(new_part, v, preferred_element_type=F32) + jnp.dot(
                old_part, stv[:, lanes], preferred_element_type=F32
            )
            att[:, lanes] = mixed.astype(BF16)
            return 0

        lax.fori_loop(first_head, first_head + heads, body, 0)

    def out_block(off, store):
        owner = xi(off)
        for i in range(2):
            zz = 2 * owner + i
            term = nt_dot(att[:, 0:OA], woa[zz].reshape(SUP, OA))
            term += nt_dot(att[:, OA:CW], wob[zz].reshape(SUP, OB))
            store(slice(i * SUP, (i + 1) * SUP), term)

    def keep_part(off):
        def store(lanes, term):
            part[off, :, lanes] = term.astype(BF16)
        return store

    def keep_own(lanes, term):
        own_part[:, lanes] = term

    half_rows = SLOT // 2
    low, high = pl.ds(0, half_rows), pl.ds(half_rows, half_rows)

    def reduce_and_finish():
        first, last = (1, "x+", low, high), (-1, "x-", high, low)
        out_block(2, keep_part(2))
        opp = {}
        for sign, dev, rows, _ in (first, last):
            opp[sign] = send_part(2, rows, rs_in.at[0, rows], devs[dev])
        out_block(1, keep_part(1))
        out_block(3, keep_part(3))
        tail = []
        for sign, dev, rows, others in (first, last):
            tail.append(send_part(1 if sign == 1 else 3, others, rs_in.at[1 if sign == 1 else 2, others], devs[dev]))
        for sign, dev, rows, others in (first, last):
            opp[sign].wait_recv()
            slot = 1 if sign == 1 else 3
            part[slot, rows, :] = (part[slot, rows, :].astype(F32) + rs_in[0, rows, :].astype(F32)).astype(BF16)
            tail.append(send_part(slot, rows, rs_in.at[1 if sign == 1 else 2, rows], devs[dev]))
        out_block(0, keep_own)
        for incoming in tail:
            incoming.wait_recv()
        lanes_own = pl.ds(pl.multiple_of(x * CW, CW), CW)

        def body(i, _):
            rows = pl.ds(pl.multiple_of(i * 16, 16), 16)
            branch = own_part[rows, :] + rs_in[1, rows, :].astype(F32) + rs_in[2, rows, :].astype(F32)
            updated = xbuf[x, rows, :].astype(F32) + modv[2, 0:1, lanes_own] * branch
            pos = lax.broadcasted_iota(jnp.int32, (16, 1), 0) + i * 16
            value = jnp.where(pos < e3, updated, 0.0).astype(BF16)
            res[rows, :] = value
            return 0

        lax.fori_loop(0, SLOT // 16, body, 0)

    def send_part(slot, rows, landing, device):
        return links.start(part.at[slot, rows], landing, device, target=landing)

    local[0].wait()

    @pl.when(s == 1)
    def _():
        pl.semaphore_wait(gate_sem, 1)

    qkv.zb_send(0)
    qkv.ya_own()
    qkv.yb_own(0)
    modulation()
    qkv.ya_relay()
    qkv.zb_send(1)
    qkv.yb_own(-1)
    qkv.yb_own(1)
    qkv.yb_relay(0)
    qkv.ya_fin()
    qkv.za_send(0, 0)
    qkv.za_send(0, 1)
    qkv.zb_send(2)
    qkv.yb_own(-2)
    qkv.yb_own(2)
    qkv.yb_relay(-1)
    qkv.yb_relay(1)
    qkv.za_send(1, 0)
    qkv.za_send(1, 1)
    qkv.zb_send(3)
    qkv.yb_own(-3)
    qkv.yb_own(3)
    local[1].wait()
    local[2].wait()
    out.ya_own()
    qkv.yb_relay(-2)
    qkv.yb_relay(2)
    x_start()
    qkv.za_send(2, 0)
    qkv.za_send(2, 1)
    qkv.zb_fin()
    qkv.yb_own(4)
    out.ya_relay()
    x_relay()
    qkv.za_send(3, 0)
    qkv.za_send(3, 1)
    out.zb_send(0)
    out.ya_fin()
    out.za_send(0, 0)
    out.za_send(0, 1)
    x_fin()
    layer_norm()
    for off in (0, -1, 1, -2, 2):
        qkv.yb_fin(off)
    qkv.yb_relay(-3)
    qkv.yb_relay(3)
    out.yb_own(0)
    out.zb_send(1)
    out.yb_own(-1)
    out.yb_own(1)
    project((0, -1, 1, -2, 2), True)
    qkv.yb_relay(4)
    out.za_send(1, 0)
    out.za_send(1, 1)
    out.zb_send(2)
    out.yb_own(-2)
    out.yb_own(2)
    qkv.za_fin()
    for off in (-3, 3, 4):
        qkv.yb_fin(off)
    project((-3, 3, 4), False)
    for off in (0, -1, 1):
        out.yb_relay(off)
    out.zb_send(3)
    out.yb_own(-3)
    out.yb_own(3)
    local[4].wait()
    local[5].wait()
    attend(0, 2)
    out.za_send(2, 0)
    out.za_send(2, 1)
    out.zb_fin()
    out.yb_own(4)
    for off in (-2, 2):
        out.yb_relay(off)
    attend(2, 2)
    out.za_send(3, 0)
    out.za_send(3, 1)

    @pl.when(s == 0)
    def _():
        pl.semaphore_signal(gate_sem, inc=1, device_id=devs["mate"], device_id_type=MESH)

    for off in (-3, 3, 4):
        out.yb_relay(off)
    attend(4, 2)
    for off in (0, -1, 1, -2, 2, -3, 3, 4):
        out.yb_fin(off)
    out.za_fin()
    reduce_and_finish()

    to_mate = links.copy(handed, res, xbuf.at[x], devs["mate"])

    @pl.when(s == 0)
    def _():
        to_mate.start()

    result_ref[...] = res[...]

    @pl.when(s == 0)
    def _():
        to_mate.wait_send()

    for copy in links.started:
        copy.wait_send()


def shards(
    hidden_in, patch_ends, timestep, mod_weight, qkv_weight, out_weight, stale_keys, stale_values
):
    feats = jnp.broadcast_to(embed_time(timestep), (16, FREQ))
    mod_mat = jnp.swapaxes(mod_weight[0], 0, 1)
    qkv_mat = jnp.swapaxes(qkv_weight[0], 0, 1)
    out_mat = jnp.swapaxes(out_weight[0], 0, 1)
    anywhere = pl.BlockSpec(memory_space=pl.ANY)
    result = pl.pallas_call(
        kernel,
        out_shape=jax.ShapeDtypeStruct((SLOT, CW), BF16),
        in_specs=[
            pl.BlockSpec(memory_space=pltpu.SMEM),
            pl.BlockSpec(memory_space=pltpu.VMEM),
        ] + [anywhere] * 6,
        out_specs=pl.BlockSpec(memory_space=pltpu.VMEM),
        scratch_shapes=[
            pltpu.VMEM((3, NZ, NY, KB, CW), BF16),
            pltpu.VMEM((NZ, NY, KB, OA), BF16),
            pltpu.VMEM((NZ, NY, KB, OB), BF16),
            pltpu.VMEM((3, FREQ, NX * CW), BF16),
            pltpu.VMEM((3, 16, NX * CW), F32),
            pltpu.VMEM((NX, SLOT, CW), BF16),
            pltpu.VMEM((NZ, SLOT, SUP), BF16),
            pltpu.VMEM((3, SLOT, CW), F32),
            pltpu.VMEM((SLOT, CW), BF16),
            pltpu.VMEM((SLOT, CW), BF16),
            pltpu.VMEM((SLOT, CW), BF16),
            pltpu.VMEM((NX, SLOT, CW), BF16),
            pltpu.VMEM((SLOT, CW), F32),
            pltpu.VMEM((3, SLOT, CW), BF16),
            pltpu.VMEM((SLOT, CW), BF16),
            pltpu.SemaphoreType.DMA((N_SEM,)),
            pltpu.SemaphoreType.DMA((N_SEM,)),
            pltpu.SemaphoreType.DMA((8,)),
            pltpu.SemaphoreType.REGULAR,
        ],
        compiler_params=pltpu.CompilerParams(
            collective_id=0, has_side_effects=True, vmem_limit_bytes=62 * 1024 * 1024
        ),
        name="patch_layers",
    )(
        patch_ends, feats, hidden_in[0], mod_mat, qkv_mat, out_mat,
        stale_keys[0, 0], stale_values[0, 0],
    )
    return result[None, None]


def solution(mesh):
    return jax.shard_map(
        shards,
        mesh=mesh,
        in_specs=(
            P("row", None, "col"),
            P("row", None),
            P("row"),
            P("section", None, None, None),
            P("section", "row", None, "col"),
            P("section", "col", "row"),
            P("section", "row", None, "col"),
            P("section", "row", None, "col"),
        ),
        out_specs=P("section", "row", None, "col"),
        check_vma=False,
    )
```

```python
import functools
import math

import jax
import jax.numpy as jnp
from jax import lax
from jax.experimental import pallas as pl
from jax.experimental.pallas import tpu as pltpu
from jax.sharding import PartitionSpec as P

HD = 128
FREQ = 256
NX, NY, NZ = 4, 4, 8
KB = 96
CW = 768
SUP = NY * KB
SLOT = 256
HEADS = CW // HD
OA = 512
OB = CW - OA
MESH = pl.DeviceIdType.MESH
F32 = jnp.float32
BF16 = jnp.bfloat16
N_SEM = 128


def embed_time(timestep):
    half_width = FREQ // 2
    frequency = jnp.exp(
        jnp.arange(half_width, dtype=F32) * (-math.log(10000.0) / half_width)
    )
    angles = timestep.astype(F32)[:, None] * frequency[None, :]
    return jnp.concatenate([jnp.cos(angles), jnp.sin(angles)], axis=1).astype(BF16)


class Links:
    def __init__(self, send_sem, recv_sem):
        self.send_sem, self.recv_sem = send_sem, recv_sem
        self.count = 0
        self.started = []

    def slot(self):
        self.count += 1
        return self.count - 1

    def copy(self, index, source, target, device):
        return pltpu.make_async_remote_copy(
            src_ref=source, dst_ref=target, send_sem=self.send_sem.at[index],
            recv_sem=self.recv_sem.at[index], device_id=device, device_id_type=MESH,
        )

    def start(self, out_view, in_view, device, target=None):
        index = self.slot()
        outgoing = self.copy(index, out_view, out_view if target is None else target, device)
        outgoing.start()
        self.started.append(outgoing)
        return self.copy(index, in_view, in_view, device)


class Gather:
    def __init__(self, links, pos, devs, views):
        self.links, self.devs = links, devs
        self.y, self.z = pos
        self.a_shard, self.a_half, self.a_sup, self.b_shard, self.b_half = views
        self.inc = {}

    def zi(self, off):
        return lax.rem(self.z + (off + NZ), NZ)

    def yi(self, off):
        return lax.rem(self.y + (off + NY), NY)

    def go(self, key, out_view, in_view, device):
        self.inc[key] = self.links.start(out_view, in_view, self.devs[device])

    def wait(self, *key):
        self.inc.pop(key).wait_recv()

    def dev(self, axis, sign):
        return axis + ("+" if sign == 1 else "-")

    def ya_own(self):
        for sign in (1, -1):
            self.go(("ya", sign), self.a_shard(self.z, self.y), self.a_shard(self.z, self.yi(-sign)), self.dev("y", sign))

    def ya_relay(self, sign):
        half = 0 if sign == 1 else 1
        self.wait("ya", sign)
        self.go(("yah", sign), self.a_half(self.z, self.yi(-sign), half), self.a_half(self.z, self.yi(-2 * sign), half), self.dev("y", sign))

    def zb_own(self, sign):
        self.zb_send(sign, 0)

    def zb_relay(self, sign, d):
        self.wait("zb", sign, d - 1)
        self.zb_send(sign, d)

    def zb_send(self, sign, d):
        here, there = self.zi(-sign * d), self.zi(-sign * (d + 1))
        if d < NZ // 2 - 1:
            views = self.b_shard(here, self.y), self.b_shard(there, self.y)
        else:
            half = 0 if sign == 1 else 1
            views = self.b_half(here, self.y, half), self.b_half(there, self.y, half)
        self.go(("zb", sign, d), *views, self.dev("z", sign))

    def yb_own(self, off):
        if off == NZ // 2:
            for sign in (1, -1):
                self.wait("zb", sign, off - 1)
        for sign in (1, -1):
            self.go(("yb", off, sign), self.b_shard(self.zi(off), self.y), self.b_shard(self.zi(off), self.yi(-sign)), self.dev("y", sign))

    def yb_relay(self, off, sign):
        half = 0 if sign == 1 else 1
        self.wait("yb", off, sign)
        self.go(("ybh", off, sign), self.b_half(self.zi(off), self.yi(-sign), half), self.b_half(self.zi(off), self.yi(-2 * sign), half), self.dev("y", sign))

    def yb_fin(self, off):
        for sign in (1, -1):
            self.wait("ybh", off, sign)

    def za_own(self, half):
        if half == 0:
            for sign in (1, -1):
                self.wait("yah", sign)
        for sign in (1, -1):
            self.za_send(sign, 0, half)

    def za_relay(self, sign, d, half):
        self.wait("za", sign, d - 1, half)
        self.za_send(sign, d, half)

    def za_send(self, sign, d, half):
        here, there = self.zi(-sign * d), self.zi(-sign * (d + 1))
        self.go(("za", sign, d, half), self.a_sup(here, half), self.a_sup(there, half), self.dev("z", sign))

    def za_fin(self):
        last = NZ // 2 - 1
        for sign, half in ((1, 1), (-1, 0)):
            self.wait("za", sign, last - 1, half)
        for sign, half in ((1, 0), (-1, 1)):
            self.wait("za", sign, last, half)


def nt_dot(left, right):
    return lax.dot_general(left, right, (((1,), (1,)), ((), ())), preferred_element_type=F32)


def kernel(
    ends_ref, feats_ref, hidden_hbm, mod_hbm, qkv_hbm, out_hbm, keys_hbm, values_hbm,
    result_ref,
    wbuf, woa, wob, modw, modv, xbuf, xm, acc, stk, stv, att, part, own_part, rs_in, res,
    send_sem, recv_sem, local_sem, gate_sem,
):
    s = lax.axis_index("section")
    row = lax.axis_index("row")
    x = lax.axis_index("col")
    z, y = row // NY, lax.rem(row, NY)

    def zy(zz, yy):
        return lax.rem(zz + NZ, NZ) * NY + lax.rem(yy + NY, NY)

    def xi(off):
        return lax.rem(x + (off + NX), NX)

    devs = {
        "y+": (s, zy(z, y + 1), x), "y-": (s, zy(z, y - 1), x),
        "z+": (s, zy(z + 1, y), x), "z-": (s, zy(z - 1, y), x),
        "x+": (s, row, xi(1)), "x-": (s, row, xi(-1)),
        "mate": (1 - s, row, x),
    }
    local = [
        pltpu.make_async_copy(qkv_hbm, wbuf.at[:, z, y], local_sem.at[0]),
        pltpu.make_async_copy(out_hbm.at[:, pl.ds(0, OA)], woa.at[z, y], local_sem.at[1]),
        pltpu.make_async_copy(out_hbm.at[:, pl.ds(OA, OB)], wob.at[z, y], local_sem.at[2]),
        pltpu.make_async_copy(mod_hbm, modw, local_sem.at[3]),
        pltpu.make_async_copy(keys_hbm, stk, local_sem.at[4]),
        pltpu.make_async_copy(values_hbm, stv, local_sem.at[5]),
    ]
    for copy in local:
        copy.start()
    load_x = pltpu.make_async_copy(hidden_hbm, xbuf.at[x], local_sem.at[6])

    @pl.when(s == 0)
    def _():
        load_x.start()

    barrier = pltpu.get_barrier_semaphore()
    for device in devs.values():
        pl.semaphore_signal(barrier, inc=1, device_id=device, device_id_type=MESH)
    pl.semaphore_wait(barrier, len(devs))

    links = Links(send_sem, recv_sem)
    qkv = Gather(links, (y, z), devs, (
        lambda zz, yy: wbuf.at[0, zz, yy],
        lambda zz, yy, h: wbuf.at[0, zz, yy, pl.ds(h * (KB // 2), KB // 2)],
        lambda zz, h: wbuf.at[0, zz, pl.ds(2 * h, 2)],
        lambda zz, yy: wbuf.at[pl.ds(1, 2), zz, yy],
        lambda zz, yy, h: wbuf.at[1 + h, zz, yy],
    ))
    out = Gather(links, (y, z), devs, (
        lambda zz, yy: woa.at[zz, yy],
        lambda zz, yy, h: woa.at[zz, yy, pl.ds(h * (KB // 2), KB // 2)],
        lambda zz, h: woa.at[zz, pl.ds(2 * h, 2)],
        lambda zz, yy: wob.at[zz, yy],
        lambda zz, yy, h: wob.at[zz, yy, pl.ds(h * (KB // 2), KB // 2)],
    ))

    handed = links.slot()
    inc = {}

    def x_start():
        @pl.when(s == 0)
        def _():
            load_x.wait()

        @pl.when(s == 1)
        def _():
            links.copy(handed, res, xbuf.at[x], devs["mate"]).wait_recv()

        for sign, dev in ((1, "x+"), (-1, "x-")):
            inc["x", sign] = links.start(xbuf.at[x], xbuf.at[xi(-sign)], devs[dev])

    def x_relay():
        half_rows = SLOT // 2
        for sign, dev, half in ((1, "x+", 0), (-1, "x-", 1)):
            rows = pl.ds(half * half_rows, half_rows)
            inc["x", sign].wait_recv()
            inc["xh", sign] = links.start(xbuf.at[xi(-sign), rows], xbuf.at[xi(-2 * sign), rows], devs[dev])

    def x_fin():
        for sign in (1, -1):
            inc["xh", sign].wait_recv()

    def modulation():
        local[3].wait()

        def body(j, _):
            modv[j] = jnp.dot(feats_ref[...], modw[j], preferred_element_type=F32)
            return 0

        lax.fori_loop(0, 3, body, 0)

    def layer_norm():
        width = NX * CW

        def body(i, _):
            rows = pl.ds(pl.multiple_of(i * 16, 16), 16)
            parts = [xbuf[c, rows, :].astype(F32) for c in range(NX)]
            total = sum(jnp.sum(p, axis=-1, keepdims=True) for p in parts)
            squares = sum(jnp.sum(p * p, axis=-1, keepdims=True) for p in parts)
            mean = total / width
            var = squares / width - mean * mean
            inv = 1.0 / jnp.sqrt(var + 1e-06)
            for b in range(NZ):
                lanes = pl.ds(b * SUP, SUP)
                piece = parts[b // 2][:, (b % 2) * SUP:(b % 2 + 1) * SUP]
                normed = (piece - mean) * inv
                xm[b, rows, :] = (normed * (1.0 + modv[1, 0:1, lanes]) + modv[0, 0:1, lanes]).astype(BF16)
            return 0

        lax.fori_loop(0, SLOT // 16, body, 0)

    def project(offs, first):
        def body(t, _):
            j = t // 3
            lanes = pl.ds(pl.multiple_of(lax.rem(t, 3) * 256, 256), 256)
            total = None
            for off in offs:
                zz = qkv.zi(off)
                block = wbuf[j, zz, :, :, lanes].reshape(SUP, 256)
                term = jnp.dot(xm[zz], block, preferred_element_type=F32)
                total = term if total is None else total + term
            if first:
                acc[j, :, lanes] = total
            else:
                acc[j, :, lanes] += total
            return 0

        lax.fori_loop(0, 9, body, 0)

    e0, e1, e2, e3 = (ends_ref[0, m] for m in range(4))
    q_pos = lax.broadcasted_iota(jnp.int32, (SLOT, 1), 0)
    limit = jnp.where(q_pos < e0, e0, jnp.where(q_pos < e1, e1, jnp.where(q_pos < e2, e2, e3)))

    def attend(first_head, heads):
        def body(h, _):
            lanes = pl.ds(pl.multiple_of(h * HD, HD), HD)
            k_pos = lax.broadcasted_iota(jnp.int32, (SLOT, SLOT), 1)
            fresh = k_pos < limit
            ok = k_pos < e3

            def norm(raw):
                return (raw * (1.0 / jnp.sqrt(jnp.mean(raw * raw, axis=-1, keepdims=True) + 1e-06))).astype(BF16)

            q = norm(acc[0, :, lanes])
            k = norm(acc[1, :, lanes])
            v = acc[2, :, lanes].astype(BF16)
            scores = jnp.where(fresh, nt_dot(q, k), nt_dot(q, stk[:, lanes])) * (1.0 / math.sqrt(HD))
            weights = jnp.where(ok, jnp.exp(scores), 0.0)
            weights = weights * (1.0 / jnp.sum(weights, axis=-1, keepdims=True))
            new_part = jnp.where(fresh, weights, 0.0).astype(BF16)
            old_part = jnp.where(fresh, 0.0, weights).astype(BF16)
            mixed = jnp.dot(new_part, v, preferred_element_type=F32) + jnp.dot(
                old_part, stv[:, lanes], preferred_element_type=F32
            )
            att[:, lanes] = mixed.astype(BF16)
            return 0

        lax.fori_loop(first_head, first_head + heads, body, 0)

    def out_block(off, store):
        owner = xi(off)
        for i in range(2):
            zz = 2 * owner + i
            term = nt_dot(att[:, 0:OA], woa[zz].reshape(SUP, OA))
            term += nt_dot(att[:, OA:CW], wob[zz].reshape(SUP, OB))
            store(slice(i * SUP, (i + 1) * SUP), term)

    def keep_part(off):
        def store(lanes, term):
            part[off, :, lanes] = term.astype(BF16)
        return store

    def keep_own(lanes, term):
        own_part[:, lanes] = term

    half_rows = SLOT // 2
    low, high = pl.ds(0, half_rows), pl.ds(half_rows, half_rows)

    def reduce_and_finish():
        first, last = (1, "x+", low, high), (-1, "x-", high, low)
        out_block(2, keep_part(2))
        opp = {}
        for sign, dev, rows, _ in (first, last):
            opp[sign] = send_part(2, rows, rs_in.at[0, rows], devs[dev])
        out_block(1, keep_part(1))
        out_block(3, keep_part(3))
        tail = []
        for sign, dev, rows, others in (first, last):
            tail.append(send_part(1 if sign == 1 else 3, others, rs_in.at[1 if sign == 1 else 2, others], devs[dev]))
        for sign, dev, rows, others in (first, last):
            opp[sign].wait_recv()
            slot = 1 if sign == 1 else 3
            part[slot, rows, :] = (part[slot, rows, :].astype(F32) + rs_in[0, rows, :].astype(F32)).astype(BF16)
            tail.append(send_part(slot, rows, rs_in.at[1 if sign == 1 else 2, rows], devs[dev]))
        out_block(0, keep_own)
        for incoming in tail:
            incoming.wait_recv()
        lanes_own = pl.ds(pl.multiple_of(x * CW, CW), CW)

        def body(i, _):
            rows = pl.ds(pl.multiple_of(i * 16, 16), 16)
            branch = own_part[rows, :] + rs_in[1, rows, :].astype(F32) + rs_in[2, rows, :].astype(F32)
            updated = xbuf[x, rows, :].astype(F32) + modv[2, 0:1, lanes_own] * branch
            pos = lax.broadcasted_iota(jnp.int32, (16, 1), 0) + i * 16
            value = jnp.where(pos < e3, updated, 0.0).astype(BF16)
            res[rows, :] = value
            return 0

        lax.fori_loop(0, SLOT // 16, body, 0)

    def send_part(slot, rows, landing, device):
        return links.start(part.at[slot, rows], landing, device, target=landing)

    local[0].wait()

    @pl.when(s == 1)
    def _():
        pl.semaphore_wait(gate_sem, 1)

    qkv.ya_own()
    qkv.zb_own(1)
    qkv.zb_own(-1)
    local[1].wait()
    local[2].wait()
    out.ya_own()
    qkv.yb_own(0)
    out.zb_own(1)
    out.zb_own(-1)
    modulation()
    out.yb_own(0)
    qkv.ya_relay(1)
    qkv.ya_relay(-1)
    out.ya_relay(1)
    out.ya_relay(-1)
    qkv.zb_relay(1, 1)
    qkv.zb_relay(-1, 1)
    qkv.yb_own(-1)
    out.zb_relay(1, 1)
    out.zb_relay(-1, 1)
    qkv.yb_relay(0, 1)
    qkv.yb_relay(0, -1)
    qkv.za_own(0)
    qkv.za_own(1)
    qkv.yb_own(1)
    qkv.zb_relay(1, 2)
    qkv.zb_relay(-1, 2)
    qkv.yb_relay(-1, 1)
    qkv.yb_relay(-1, -1)
    qkv.yb_own(-2)
    qkv.za_relay(1, 1, 0)
    qkv.za_relay(-1, 1, 0)
    qkv.yb_relay(1, 1)
    qkv.yb_relay(1, -1)
    qkv.za_relay(1, 1, 1)
    qkv.za_relay(-1, 1, 1)
    qkv.yb_own(2)
    qkv.zb_relay(1, 3)
    qkv.zb_relay(-1, 3)
    qkv.yb_relay(-2, 1)
    qkv.yb_relay(-2, -1)
    qkv.za_relay(1, 2, 0)
    qkv.za_relay(-1, 2, 0)
    qkv.yb_own(-3)
    qkv.za_relay(1, 2, 1)
    qkv.za_relay(-1, 2, 1)
    qkv.yb_relay(2, 1)
    qkv.yb_relay(2, -1)
    qkv.yb_own(3)
    out.za_own(0)
    qkv.yb_relay(-3, 1)
    qkv.yb_relay(-3, -1)
    qkv.za_relay(1, 3, 0)
    out.zb_relay(-1, 2)
    x_start()
    qkv.yb_own(4)
    qkv.za_relay(-1, 3, 1)
    out.zb_relay(1, 2)
    out.za_own(1)
    qkv.yb_relay(3, 1)
    qkv.yb_relay(3, -1)
    out.zb_relay(-1, 3)
    out.za_relay(1, 1, 0)
    out.za_relay(-1, 1, 0)
    out.yb_relay(0, 1)
    out.yb_relay(0, -1)
    out.yb_own(-1)
    out.yb_own(1)
    x_relay()
    out.yb_own(-2)
    out.zb_relay(1, 3)
    out.yb_own(2)
    out.yb_own(-3)
    qkv.yb_relay(4, 1)
    qkv.yb_relay(4, -1)

    @pl.when(s == 0)
    def _():
        pl.semaphore_signal(gate_sem, inc=1, device_id=devs["mate"], device_id_type=MESH)

    out.za_relay(1, 1, 1)
    out.za_relay(-1, 1, 1)
    out.yb_own(3)
    x_fin()
    layer_norm()
    out.yb_relay(-1, 1)
    out.yb_relay(-1, -1)
    out.yb_relay(1, 1)
    out.yb_relay(1, -1)
    out.za_relay(1, 2, 0)
    qkv.yb_fin(0)
    qkv.yb_fin(-1)
    qkv.yb_fin(1)
    qkv.yb_fin(-2)
    qkv.yb_fin(2)
    project((0, -1, 1, -2, 2), True)
    out.yb_relay(-2, 1)
    out.yb_relay(-2, -1)
    out.yb_own(4)
    out.za_relay(-1, 2, 0)
    out.yb_relay(2, 1)
    out.yb_relay(2, -1)
    out.yb_relay(-3, 1)
    out.yb_relay(-3, -1)
    out.za_relay(1, 2, 1)
    out.za_relay(-1, 2, 1)
    qkv.za_fin()
    qkv.yb_fin(-3)
    qkv.yb_fin(3)
    qkv.yb_fin(4)
    project((-3, 3, 4), False)
    out.yb_relay(3, 1)
    out.yb_relay(3, -1)
    local[4].wait()
    local[5].wait()
    attend(0, 2)
    out.za_relay(1, 3, 0)
    out.yb_relay(4, 1)
    out.yb_relay(4, -1)
    attend(2, 2)
    attend(4, 2)
    out.za_relay(-1, 3, 1)
    out.yb_fin(0)
    out.yb_fin(-1)
    out.yb_fin(1)
    out.yb_fin(-2)
    out.yb_fin(2)
    out.yb_fin(-3)
    out.yb_fin(3)
    out.yb_fin(4)
    out.za_fin()
    reduce_and_finish()

    to_mate = links.copy(handed, res, xbuf.at[x], devs["mate"])

    @pl.when(s == 0)
    def _():
        to_mate.start()

    result_ref[...] = res[...]

    @pl.when(s == 0)
    def _():
        to_mate.wait_send()

    for copy in links.started:
        copy.wait_send()


def shards(
    hidden_in, patch_ends, timestep, mod_weight, qkv_weight, out_weight, stale_keys, stale_values
):
    feats = jnp.broadcast_to(embed_time(timestep), (16, FREQ))
    mod_mat = jnp.swapaxes(mod_weight[0], 0, 1)
    qkv_mat = jnp.swapaxes(qkv_weight[0], 0, 1)
    out_mat = jnp.swapaxes(out_weight[0], 0, 1)
    anywhere = pl.BlockSpec(memory_space=pl.ANY)
    result = pl.pallas_call(
        kernel,
        out_shape=jax.ShapeDtypeStruct((SLOT, CW), BF16),
        in_specs=[
            pl.BlockSpec(memory_space=pltpu.SMEM),
            pl.BlockSpec(memory_space=pltpu.VMEM),
        ] + [anywhere] * 6,
        out_specs=pl.BlockSpec(memory_space=pltpu.VMEM),
        scratch_shapes=[
            pltpu.VMEM((3, NZ, NY, KB, CW), BF16),
            pltpu.VMEM((NZ, NY, KB, OA), BF16),
            pltpu.VMEM((NZ, NY, KB, OB), BF16),
            pltpu.VMEM((3, FREQ, NX * CW), BF16),
            pltpu.VMEM((3, 16, NX * CW), F32),
            pltpu.VMEM((NX, SLOT, CW), BF16),
            pltpu.VMEM((NZ, SLOT, SUP), BF16),
            pltpu.VMEM((3, SLOT, CW), F32),
            pltpu.VMEM((SLOT, CW), BF16),
            pltpu.VMEM((SLOT, CW), BF16),
            pltpu.VMEM((SLOT, CW), BF16),
            pltpu.VMEM((NX, SLOT, CW), BF16),
            pltpu.VMEM((SLOT, CW), F32),
            pltpu.VMEM((3, SLOT, CW), BF16),
            pltpu.VMEM((SLOT, CW), BF16),
            pltpu.SemaphoreType.DMA((N_SEM,)),
            pltpu.SemaphoreType.DMA((N_SEM,)),
            pltpu.SemaphoreType.DMA((8,)),
            pltpu.SemaphoreType.REGULAR,
        ],
        compiler_params=pltpu.CompilerParams(
            collective_id=0, has_side_effects=True, vmem_limit_bytes=62 * 1024 * 1024
        ),
        name="patch_layers",
    )(
        patch_ends, feats, hidden_in[0], mod_mat, qkv_mat, out_mat,
        stale_keys[0, 0], stale_values[0, 0],
    )
    return result[None, None]


def solution(mesh):
    return jax.shard_map(
        shards,
        mesh=mesh,
        in_specs=(
            P("row", None, "col"),
            P("row", None),
            P("row"),
            P("section", None, None, None),
            P("section", "row", None, "col"),
            P("section", "col", "row"),
            P("section", "row", None, "col"),
            P("section", "row", None, "col"),
        ),
        out_specs=P("section", "row", None, "col"),
        check_vma=False,
    )
```

```python
import functools
import math

import jax
import jax.numpy as jnp
from jax import lax
from jax.experimental import pallas as pl
from jax.experimental.pallas import tpu as pltpu
from jax.sharding import PartitionSpec as P

HD = 128
FREQ = 256
NX, NY, NZ = 4, 4, 8
KB = 96
CW = 768
SUP = NY * KB
SLOT = 256
HEADS = CW // HD
OA = 512
OB = CW - OA
OA2, OB2 = OA // 2, OB // 2
MESH = pl.DeviceIdType.MESH
F32 = jnp.float32
BF16 = jnp.bfloat16
N_SEM = 160


def embed_time(timestep):
    half_width = FREQ // 2
    frequency = jnp.exp(
        jnp.arange(half_width, dtype=F32) * (-math.log(10000.0) / half_width)
    )
    angles = timestep.astype(F32)[:, None] * frequency[None, :]
    return jnp.concatenate([jnp.cos(angles), jnp.sin(angles)], axis=1).astype(BF16)


class Links:
    def __init__(self, send_sem, recv_sem):
        self.send_sem, self.recv_sem = send_sem, recv_sem
        self.count = 0
        self.started = []

    def slot(self):
        self.count += 1
        return self.count - 1

    def copy(self, index, source, target, device):
        return pltpu.make_async_remote_copy(
            src_ref=source, dst_ref=target, send_sem=self.send_sem.at[index],
            recv_sem=self.recv_sem.at[index], device_id=device, device_id_type=MESH,
        )

    def start(self, out_view, in_view, device, target=None):
        index = self.slot()
        outgoing = self.copy(index, out_view, out_view if target is None else target, device)
        outgoing.start()
        self.started.append(outgoing)
        return self.copy(index, in_view, in_view, device)


class Gather:
    def __init__(self, links, pos, devs, views):
        self.links, self.devs = links, devs
        self.y, self.z = pos
        self.a_shard, self.a_half, self.a_sup, self.b_shard, self.b_half = views
        self.inc = {}

    def zi(self, off):
        return lax.rem(self.z + (off + NZ), NZ)

    def yi(self, off):
        return lax.rem(self.y + (off + NY), NY)

    def go(self, key, out_view, in_view, device):
        self.inc[key] = self.links.start(out_view, in_view, self.devs[device])

    def wait(self, *key):
        self.inc.pop(key).wait_recv()

    def dev(self, axis, sign):
        return axis + ("+" if sign == 1 else "-")

    def ya_own(self):
        for sign in (1, -1):
            self.go(("ya", sign), self.a_shard(self.z, self.y), self.a_shard(self.z, self.yi(-sign)), self.dev("y", sign))

    def ya_relay(self, sign):
        half = 0 if sign == 1 else 1
        self.wait("ya", sign)
        self.go(("yah", sign), self.a_half(self.z, self.yi(-sign), half), self.a_half(self.z, self.yi(-2 * sign), half), self.dev("y", sign))

    def zb_own(self, sign):
        self.zb_send(sign, 0)

    def zb_relay(self, sign, d):
        self.wait("zb", sign, d - 1)
        self.zb_send(sign, d)

    def zb_send(self, sign, d):
        here, there = self.zi(-sign * d), self.zi(-sign * (d + 1))
        if d < NZ // 2 - 1:
            views = self.b_shard(here, self.y), self.b_shard(there, self.y)
        else:
            half = 0 if sign == 1 else 1
            views = self.b_half(here, self.y, half), self.b_half(there, self.y, half)
        self.go(("zb", sign, d), *views, self.dev("z", sign))

    def yb_own(self, off):
        if off == NZ // 2:
            for sign in (1, -1):
                self.wait("zb", sign, off - 1)
        for sign in (1, -1):
            self.go(("yb", off, sign), self.b_shard(self.zi(off), self.y), self.b_shard(self.zi(off), self.yi(-sign)), self.dev("y", sign))

    def yb_relay(self, off, sign):
        half = 0 if sign == 1 else 1
        self.wait("yb", off, sign)
        self.go(("ybh", off, sign), self.b_half(self.zi(off), self.yi(-sign), half), self.b_half(self.zi(off), self.yi(-2 * sign), half), self.dev("y", sign))

    def za_own(self, half):
        if half == 0:
            for sign in (1, -1):
                self.wait("yah", sign)
        for sign in (1, -1):
            self.za_send(sign, 0, half)

    def za_relay(self, sign, d, half):
        self.wait("za", sign, d - 1, half)
        self.za_send(sign, d, half)

    def za_send(self, sign, d, half):
        here, there = self.zi(-sign * d), self.zi(-sign * (d + 1))
        self.go(("za", sign, d, half), self.a_sup(here, half), self.a_sup(there, half), self.dev("z", sign))

    def fin(self, off):
        for sign in (1, -1):
            self.wait("ybh", off, sign)
        for key in [k for k in self.inc if k[0] == "za" and -k[1] * (k[2] + 1) % NZ == off % NZ]:
            self.wait(*key)


class PairGather:
    def __init__(self, links, pos, devs, views):
        self.links, self.devs = links, devs
        self.y, self.z = pos
        self.mate_y = NY - 1 - self.y
        self.near_y = self.y + 1 - 2 * lax.rem(self.y, 2)
        self.source, self.landing, self.a_slot, self.a_sup, self.b_slot = views
        self.inc = {}

    def zi(self, off):
        return lax.rem(self.z + (off + NZ), NZ)

    def slot(self, k):
        return self.y if k == 0 else self.mate_y

    def near_slot(self, k):
        return self.near_y if k == 0 else NY - 1 - self.near_y

    def go(self, key, out_view, in_view, device, target=None):
        self.inc[key] = self.links.start(out_view, in_view, self.devs[device], target)

    def wait(self, *key):
        self.inc.pop(key).wait_recv()

    def inject(self):
        for i, (source, target) in enumerate(zip(self.source, self.landing(self.y))):
            self.go(("inj", i), source, self.landing(self.mate_y)[i], "pair", target)

    def injected(self):
        for i in range(len(self.source)):
            if ("inj", i) in self.inc:
                self.wait("inj", i)

    def ya_own(self, k):
        if k == 1:
            self.injected()
        self.go(("ya", k), self.a_slot(self.z, self.slot(k)), self.a_slot(self.z, self.near_slot(k)), "near")

    def za_own(self, half):
        if half == 0:
            for k in range(2):
                self.wait("ya", k)
        for sign in (1, -1):
            self.za_send(sign, 0, half)

    def za_relay(self, sign, d, half):
        self.wait("za", sign, d - 1, half)
        self.za_send(sign, d, half)

    def za_send(self, sign, d, half):
        here, there = self.zi(-sign * d), self.zi(-sign * (d + 1))
        self.go(("za", sign, d, half), self.a_sup(here, half), self.a_sup(there, half), "z+" if sign == 1 else "z-")

    def zb_own(self, k, sign):
        if k == 1:
            self.injected()
        self.zb_send(k, sign, 0)

    def zb_relay(self, k, sign, d):
        self.wait("zb", k, sign, d - 1)
        self.zb_send(k, sign, d)

    def zb_send(self, k, sign, d):
        here, there = self.zi(-sign * d), self.zi(-sign * (d + 1))
        self.go(("zb", k, sign, d), self.b_slot(here, self.slot(k)), self.b_slot(there, self.slot(k)), "z+" if sign == 1 else "z-")

    def yb_own(self, off, k):
        if off == 0 and k == 1:
            self.injected()
        for sign in (1, -1):
            for d in range(NZ // 2):
                if off % NZ == -sign * (d + 1) % NZ and ("zb", k, sign, d) in self.inc:
                    self.wait("zb", k, sign, d)
        self.go(("yb", off, k), self.b_slot(self.zi(off), self.slot(k)), self.b_slot(self.zi(off), self.near_slot(k)), "near")

    def fin(self, off):
        for k in range(2):
            self.wait("yb", off, k)
        self.fin_a(off)

    def fin_a(self, off):
        for key in [k for k in self.inc if k[0] == "za" and -k[1] * (k[2] + 1) % NZ == off % NZ]:
            self.wait(*key)


def nt_dot(left, right):
    return lax.dot_general(left, right, (((1,), (1,)), ((), ())), preferred_element_type=F32)


def kernel(
    ends_ref, feats_ref, marks_ref, hidden_hbm, mod_hbm, qkv_hbm, out_hbm, keys_hbm, values_hbm,
    result_ref,
    wbuf, woa, wob, modw, modv, xbuf, xm, acc, acc2, stk, stv, stk2, stv2, att, att2, part, own_part, rs_in, pair_in,
    feats_in, marks, res,
    send_sem, recv_sem, local_sem, hand_sem, gate_sem,
):
    s = lax.axis_index("section")
    row = lax.axis_index("row")
    x = lax.axis_index("col")
    z, y = row // NY, lax.rem(row, NY)

    def zy(zz, yy):
        return lax.rem(zz + NZ, NZ) * NY + lax.rem(yy + NY, NY)

    def xi(off):
        return lax.rem(x + (off + NX), NX)

    devs = {
        "y+": (s, zy(z, y + 1), x), "y-": (s, zy(z, y - 1), x),
        "z+": (s, zy(z + 1, y), x), "z-": (s, zy(z - 1, y), x),
        "x+": (s, row, xi(1)), "x-": (s, row, xi(-1)),
        "mate": (1 - s, row, x),
    }
    load_mod = pltpu.make_async_copy(mod_hbm, modw, local_sem.at[3])
    load_mod.start()
    load_x = pltpu.make_async_copy(hidden_hbm, xbuf.at[0, x], local_sem.at[6])
    half_lanes = CW // 2
    group = y // 2
    mine = pl.ds(pl.multiple_of(group * half_lanes, half_lanes), half_lanes)
    other = pl.ds(pl.multiple_of((1 - group) * half_lanes, half_lanes), half_lanes)

    def out_lanes(which, size, start):
        return pl.ds(pl.multiple_of(which * half_lanes + start, HD), size)

    whole = [
        pltpu.make_async_copy(qkv_hbm, wbuf.at[:, z, y], local_sem.at[0]),
        pltpu.make_async_copy(out_hbm.at[:, pl.ds(0, OA)], woa.at[z, y], local_sem.at[1]),
        pltpu.make_async_copy(out_hbm.at[:, pl.ds(OA, OB)], wob.at[z, y], local_sem.at[2]),
        pltpu.make_async_copy(keys_hbm, stk, local_sem.at[4]),
        pltpu.make_async_copy(values_hbm, stv, local_sem.at[5]),
    ]
    halves = [
        pltpu.make_async_copy(qkv_hbm.at[:, :, mine], wbuf.at[:, z, y, :, pl.ds(0, half_lanes)], local_sem.at[0]),
        pltpu.make_async_copy(out_hbm.at[:, out_lanes(group, OA2, 0)], woa.at[z, y, :, pl.ds(0, OA2)], local_sem.at[1]),
        pltpu.make_async_copy(out_hbm.at[:, out_lanes(group, OB2, OA2)], wob.at[z, y, :, pl.ds(0, OB2)], local_sem.at[2]),
        pltpu.make_async_copy(keys_hbm.at[:, mine], stk2.at[0], local_sem.at[4]),
        pltpu.make_async_copy(values_hbm.at[:, mine], stv2.at[0], local_sem.at[5]),
    ]

    @pl.when(s == 0)
    def _():
        for copy in halves:
            copy.start()
        load_x.start()

    @pl.when(s == 1)
    def _():
        for copy in whole:
            copy.start()

    marks[0] = marks_ref[...]

    barrier = pltpu.get_barrier_semaphore()
    for device in devs.values():
        pl.semaphore_signal(barrier, inc=1, device_id=device, device_id_type=MESH)
    pl.semaphore_wait(barrier, len(devs))

    handed = pltpu.make_async_remote_copy(
        src_ref=res, dst_ref=xbuf.at[0, x], send_sem=hand_sem.at[0], recv_sem=hand_sem.at[1],
        device_id=devs["mate"], device_id_type=MESH,
    )

    def modulation(r, feats):
        def body(j, _):
            modv[r, j] = jnp.dot(feats[...], modw[j], preferred_element_type=F32)
            return 0

        lax.fori_loop(0, 3, body, 0)

    def layer_norm(first, count):
        width = NX * CW

        def body(i, _):
            r = first * 64 // SLOT
            rows = pl.ds(pl.multiple_of(i * 16 - r * SLOT, 16), 16)
            to_rows = pl.ds(pl.multiple_of(i * 16, 16), 16)
            parts = [xbuf[r, c, rows, :].astype(F32) for c in range(NX)]
            total = sum(jnp.sum(p, axis=-1, keepdims=True) for p in parts)
            squares = sum(jnp.sum(p * p, axis=-1, keepdims=True) for p in parts)
            mean = total / width
            var = squares / width - mean * mean
            inv = 1.0 / jnp.sqrt(var + 1e-06)
            for b in range(NZ):
                lanes = pl.ds(b * SUP, SUP)
                piece = parts[b // 2][:, (b % 2) * SUP:(b % 2 + 1) * SUP]
                normed = (piece - mean) * inv
                xm[b, to_rows, :] = (normed * (1.0 + modv[r, 1, 0:1, lanes]) + modv[r, 0, 0:1, lanes]).astype(BF16)
            return 0

        lax.fori_loop(first * 4, (first + count) * 4, body, 0)

    def attend_head(q, k, v, old_k, old_v, mark):
        e0, e1, e2, e3 = (mark[0:1, m:m + 1] for m in range(4))
        q_pos = lax.broadcasted_iota(jnp.int32, (SLOT, 1), 0)
        limit = jnp.where(q_pos < e0, e0, jnp.where(q_pos < e1, e1, jnp.where(q_pos < e2, e2, e3)))
        k_pos = lax.broadcasted_iota(jnp.int32, (SLOT, SLOT), 1)
        fresh = k_pos < limit
        ok = k_pos < e3

        def norm(raw):
            return (raw * (1.0 / jnp.sqrt(jnp.mean(raw * raw, axis=-1, keepdims=True) + 1e-06))).astype(BF16)

        q, k, v = norm(q), norm(k), v.astype(BF16)
        scores = jnp.where(fresh, nt_dot(q, k), nt_dot(q, old_k)) * (1.0 / math.sqrt(HD))
        weights = jnp.where(ok, jnp.exp(scores), 0.0)
        weights = weights * (1.0 / jnp.sum(weights, axis=-1, keepdims=True))
        new_part = jnp.where(fresh, weights, 0.0).astype(BF16)
        old_part = jnp.where(fresh, 0.0, weights).astype(BF16)
        mixed = jnp.dot(new_part, v, preferred_element_type=F32) + jnp.dot(
            old_part, old_v, preferred_element_type=F32
        )
        return mixed.astype(BF16)

    e3 = ends_ref[0, 3]
    half_rows = SLOT // 2
    lanes_own = pl.ds(pl.multiple_of(x * CW, CW), CW)

    class Summed:
        def __init__(self, links, base, block):
            self.links, self.base, self.block = links, base, block
            self.low, self.high = pl.ds(base, half_rows), pl.ds(base + half_rows, half_rows)
            self.ways = ((1, "x+", self.low, self.high, 1), (-1, "x-", self.high, self.low, 3))
            self.opp, self.tail = {}, []

        def rows(self):
            return pl.ds(self.base, SLOT)

        def term(self, off):
            for i in range(2):
                value = self.block(2 * xi(off) + i)
                if off == 0:
                    own_part[self.rows(), i * SUP:(i + 1) * SUP] = value
                else:
                    part[off, self.rows(), i * SUP:(i + 1) * SUP] = value.astype(BF16)

        def far(self):
            self.term(2)
            for sign, dev, rows, _, _ in self.ways:
                self.opp[sign] = self.links.start(part.at[2, rows], rs_in.at[0, rows], devs[dev], rs_in.at[0, rows])

        def near(self):
            self.term(1)
            self.term(3)
            for sign, dev, _, others, slot in self.ways:
                land = rs_in.at[1 if sign == 1 else 2, others]
                self.tail.append(self.links.start(part.at[slot, others], land, devs[dev], land))

        def relay(self):
            for sign, dev, rows, _, slot in self.ways:
                self.opp[sign].wait_recv()
                part[slot, rows, :] = (part[slot, rows, :].astype(F32) + rs_in[0, rows, :].astype(F32)).astype(BF16)
                land = rs_in.at[1 if sign == 1 else 2, rows]
                self.tail.append(self.links.start(part.at[slot, rows], land, devs[dev], land))

        def wait(self):
            for incoming in self.tail:
                incoming.wait_recv()

        def total(self, i):
            rows = pl.ds(pl.multiple_of(self.base + i * 16, 16), 16)
            return own_part[rows, :] + rs_in[1, rows, :].astype(F32) + rs_in[2, rows, :].astype(F32)

    def finish(summed, extra):
        def body(i, _):
            rows = pl.ds(pl.multiple_of(i * 16, 16), 16)
            branch = summed.total(i)
            if extra is not None:
                branch += extra[rows, :].astype(F32)
            updated = xbuf[0, x, rows, :].astype(F32) + modv[0, 2, 0:1, lanes_own] * branch
            pos = lax.broadcasted_iota(jnp.int32, (16, 1), 0) + i * 16
            res[rows, :] = jnp.where(pos < e3, updated, 0.0).astype(BF16)
            return 0

        lax.fori_loop(0, SLOT // 16, body, 0)

    def share_x(links, r, inc):
        def own():
            for sign, dev in ((1, "x+"), (-1, "x-")):
                inc["x", r, sign] = links.start(xbuf.at[r, x], xbuf.at[r, xi(-sign)], devs[dev])

        def relay(sign):
            rows = pl.ds(0 if sign == 1 else half_rows, half_rows)
            inc["x", r, sign].wait_recv()
            inc["xh", r, sign] = links.start(
                xbuf.at[r, xi(-sign), rows], xbuf.at[r, xi(-2 * sign), rows], devs["x+" if sign == 1 else "x-"]
            )

        def fin():
            for sign in (1, -1):
                inc["xh", r, sign].wait_recv()

        return own, relay, fin

    def open_gate():
        pl.semaphore_signal(gate_sem, inc=1, device_id=devs["mate"], device_id_type=MESH)

    @pl.when(s == 0)
    def _():
        links = Links(send_sem, recv_sem)
        mate_y = NY - 1 - y
        near_y = y + 1 - 2 * lax.rem(y, 2)
        ways = dict(devs)
        ways["pair"] = (s, z * NY + mate_y, x)
        ways["near"] = (s, z * NY + near_y, x)
        low = pl.ds(0, half_lanes)
        qkv = PairGather(links, (y, z), ways, (
            [qkv_hbm.at[:, :, other]],
            lambda yy: [wbuf.at[:, z, yy, :, low]],
            lambda zz, yy: wbuf.at[0, zz, yy, :, low],
            lambda zz, h: wbuf.at[0, zz, pl.ds(2 * h, 2), :, low],
            lambda zz, yy: wbuf.at[pl.ds(1, 2), zz, yy, :, low],
        ))
        a_low, b_low = pl.ds(0, OA2), pl.ds(0, OB2)
        out = PairGather(links, (y, z), ways, (
            [out_hbm.at[:, out_lanes(1 - group, OA2, 0)], out_hbm.at[:, out_lanes(1 - group, OB2, OA2)]],
            lambda yy: [woa.at[z, yy, :, a_low], wob.at[z, yy, :, b_low]],
            lambda zz, yy: woa.at[zz, yy, :, a_low],
            lambda zz, h: woa.at[zz, pl.ds(2 * h, 2), :, a_low],
            lambda zz, yy: wob.at[zz, yy, :, b_low],
        ))
        inc = {}
        shares = [share_x(links, r, inc) for r in range(2)]

        def send_small():
            inc["f"] = links.start(feats_ref, feats_in, ways["pair"], feats_in)
            inc["m"] = links.start(marks_ref, marks.at[1], ways["pair"], marks.at[1])

        def send_hidden():
            inc["xc"] = links.start(hidden_hbm, xbuf.at[1, x], ways["pair"], xbuf.at[1, x])

        def send_stale():
            inc["sk"] = links.start(keys_hbm.at[:, other], stk2.at[1], ways["pair"], stk2.at[1])
            inc["sv"] = links.start(values_hbm.at[:, other], stv2.at[1], ways["pair"], stv2.at[1])

        def x_own(r):
            if r == 0:
                load_x.wait()
            else:
                inc["xc"].wait_recv()
            shares[r][0]()

        def x_relay(r, sign):
            shares[r][1](sign)

        def modulations():
            load_mod.wait()
            modulation(0, feats_ref)
            inc["f"].wait_recv()
            modulation(1, feats_in)

        def project(offs, first):
            def body(t, _):
                j = t // 2
                rows = pl.ds(pl.multiple_of(lax.rem(t, 2) * SLOT, SLOT), SLOT)
                total = None
                for off in offs:
                    zz = qkv.zi(off)
                    block = wbuf[j, zz, :, :, low].reshape(SUP, half_lanes)
                    term = jnp.dot(xm[zz, rows, :], block, preferred_element_type=F32)
                    total = term if total is None else total + term
                if first:
                    acc2[j, rows, :] = total
                else:
                    acc2[j, rows, :] += total
                return 0

            lax.fori_loop(0, 6, body, 0)

        def attend(first_item, items):
            def body(t, _):
                r = t // 3
                rows = pl.ds(pl.multiple_of(r * SLOT, SLOT), SLOT)
                lanes = pl.ds(pl.multiple_of(lax.rem(t, 3) * HD, HD), HD)
                att2[rows, lanes] = attend_head(
                    acc2[0, rows, lanes], acc2[1, rows, lanes], acc2[2, rows, lanes],
                    stk2[r, :, lanes], stv2[r, :, lanes], marks[r],
                )
                return 0

            lax.fori_loop(first_item, first_item + items, body, 0)

        def block_of(base):
            rows = pl.ds(base, SLOT)

            def block(zz):
                value = nt_dot(att2[rows, 0:OA2], woa[zz, :, :, a_low].reshape(SUP, OA2))
                return value + nt_dot(att2[rows, OA2:OA2 + OB2], wob[zz, :, :, b_low].reshape(SUP, OB2))

            return block

        def reduce_and_finish():
            theirs, ours = Summed(links, SLOT, block_of(SLOT)), Summed(links, 0, block_of(0))
            theirs.far()
            theirs.near()
            ours.far()
            theirs.relay()
            ours.near()
            theirs.term(0)
            theirs.wait()

            def body(i, _):
                att_rows = pl.ds(pl.multiple_of(i * 16, 16), 16)
                part[0, att_rows, :] = theirs.total(i).astype(BF16)
                return 0

            lax.fori_loop(0, SLOT // 16, body, 0)
            paired = links.start(part.at[0, pl.ds(0, SLOT)], pair_in, ways["pair"], pair_in)
            ours.relay()
            ours.term(0)
            ours.wait()
            paired.wait_recv()
            finish(ours, pair_in)

        halves[0].wait()
        send_small()
        qkv.inject()
        send_hidden()
        out.inject()
        send_stale()
        qkv.ya_own(0)
        qkv.zb_own(0, 1)
        qkv.zb_own(0, -1)
        halves[1].wait()
        halves[2].wait()
        out.ya_own(0)
        qkv.yb_own(0, 0)
        out.zb_own(0, 1)
        out.zb_own(0, -1)
        out.yb_own(0, 0)
        x_own(0)
        modulations()
        qkv.zb_relay(0, 1, 1)
        qkv.zb_relay(0, -1, 1)
        qkv.yb_own(-1, 0)
        qkv.yb_own(1, 0)
        out.zb_relay(0, 1, 1)
        out.zb_relay(0, -1, 1)
        out.yb_own(-1, 0)
        out.yb_own(1, 0)
        qkv.ya_own(1)
        qkv.zb_own(1, 1)
        qkv.zb_own(1, -1)
        qkv.yb_own(0, 1)
        x_relay(0, 1)
        x_relay(0, -1)
        qkv.zb_relay(0, 1, 2)
        qkv.zb_relay(0, -1, 2)
        qkv.yb_own(-2, 0)
        out.zb_relay(0, 1, 2)
        out.zb_relay(0, -1, 2)
        qkv.yb_own(2, 0)
        x_own(1)
        qkv.zb_relay(1, 1, 1)
        qkv.zb_relay(1, -1, 1)
        qkv.yb_own(-1, 1)
        out.zb_own(1, 1)
        out.zb_own(1, -1)
        qkv.za_own(0)
        qkv.za_own(1)
        shares[0][2]()
        layer_norm(0, 1)
        qkv.zb_relay(0, 1, 3)
        layer_norm(1, 1)
        out.ya_own(1)
        qkv.yb_own(-3, 0)
        layer_norm(2, 1)
        out.zb_relay(0, 1, 3)
        layer_norm(3, 1)
        qkv.zb_relay(1, 1, 2)
        qkv.zb_relay(1, -1, 2)
        out.zb_relay(1, -1, 1)
        qkv.yb_own(3, 0)
        out.zb_relay(1, 1, 1)
        qkv.za_relay(1, 1, 0)
        qkv.za_relay(-1, 1, 0)
        qkv.yb_own(1, 1)
        x_relay(1, 1)
        x_relay(1, -1)
        qkv.za_relay(1, 1, 1)
        qkv.za_relay(-1, 1, 1)
        qkv.yb_own(-2, 1)
        out.za_own(0)
        qkv.zb_relay(1, -1, 3)
        qkv.yb_own(4, 0)
        out.zb_relay(1, -1, 2)
        out.za_own(1)
        shares[1][2]()
        layer_norm(4, 1)
        layer_norm(5, 1)
        qkv.yb_own(2, 1)
        qkv.za_relay(-1, 2, 0)
        out.zb_relay(1, 1, 2)
        layer_norm(6, 1)
        layer_norm(7, 1)
        qkv.fin(0)
        project((0,), True)
        qkv.yb_own(-3, 1)
        qkv.za_relay(1, 2, 0)
        qkv.za_relay(-1, 2, 1)
        qkv.fin(-1)
        project((-1,), False)
        qkv.yb_own(3, 1)
        qkv.za_relay(1, 2, 1)
        out.za_relay(-1, 1, 0)
        qkv.fin(1)
        project((1,), False)
        qkv.fin(-2)
        project((-2,), False)
        qkv.yb_own(4, 1)
        out.zb_relay(1, -1, 3)
        out.za_relay(1, 1, 0)
        out.za_relay(1, 1, 1)
        out.za_relay(-1, 1, 1)
        out.yb_own(-2, 0)
        out.yb_own(2, 0)
        out.yb_own(-3, 0)
        qkv.fin(2)
        project((2,), False)
        qkv.za_relay(1, 3, 0)
        out.yb_own(3, 0)
        out.yb_own(4, 0)
        out.yb_own(0, 1)
        out.yb_own(-1, 1)
        out.yb_own(1, 1)
        qkv.za_relay(-1, 3, 1)
        out.yb_own(-2, 1)
        qkv.fin(-3)
        project((-3,), False)
        out.yb_own(2, 1)
        out.yb_own(-3, 1)
        out.yb_own(3, 1)
        out.za_relay(-1, 2, 0)
        out.za_relay(1, 2, 0)
        out.yb_own(4, 1)
        qkv.fin(3)
        project((3,), False)
        out.za_relay(1, 2, 1)
        out.za_relay(-1, 2, 1)
        open_gate()
        qkv.fin(4)
        project((4,), False)
        halves[3].wait()
        halves[4].wait()
        inc["sk"].wait_recv()
        inc["sv"].wait_recv()
        inc["m"].wait_recv()
        attend(0, 1)
        out.za_relay(1, 3, 0)
        attend(1, 1)
        out.za_relay(-1, 3, 1)
        attend(2, 1)
        attend(3, 1)
        attend(4, 1)
        attend(5, 1)
        out.fin(0)
        out.fin(-1)
        out.fin(1)
        out.fin(-2)
        out.fin(2)
        out.fin(-3)
        out.fin(3)
        out.fin(4)
        reduce_and_finish()
        handed.start()
        result_ref[...] = res[...]
        handed.wait_send()
        for copy in links.started:
            copy.wait_send()

    @pl.when(s == 1)
    def _():
        links = Links(send_sem, recv_sem)
        qkv = Gather(links, (y, z), devs, (
            lambda zz, yy: wbuf.at[0, zz, yy],
            lambda zz, yy, h: wbuf.at[0, zz, yy, pl.ds(h * (KB // 2), KB // 2)],
            lambda zz, h: wbuf.at[0, zz, pl.ds(2 * h, 2)],
            lambda zz, yy: wbuf.at[pl.ds(1, 2), zz, yy],
            lambda zz, yy, h: wbuf.at[1 + h, zz, yy],
        ))
        out = Gather(links, (y, z), devs, (
            lambda zz, yy: woa.at[zz, yy],
            lambda zz, yy, h: woa.at[zz, yy, pl.ds(h * (KB // 2), KB // 2)],
            lambda zz, h: woa.at[zz, pl.ds(2 * h, 2)],
            lambda zz, yy: wob.at[zz, yy],
            lambda zz, yy, h: wob.at[zz, yy, pl.ds(h * (KB // 2), KB // 2)],
        ))
        inc = {}
        share = share_x(links, 0, inc)

        def x_start():
            handed.wait_recv()
            share[0]()

        def x_relay(sign):
            share[1](sign)

        def x_fin():
            share[2]()

        def modulations():
            load_mod.wait()
            modulation(0, feats_ref)

        rows = pl.ds(0, SLOT)

        def project(offs, first):
            def body(t, _):
                j = t // 3
                lanes = pl.ds(pl.multiple_of(lax.rem(t, 3) * 256, 256), 256)
                total = None
                for off in offs:
                    zz = qkv.zi(off)
                    block = wbuf[j, zz, :, :, lanes].reshape(SUP, 256)
                    term = jnp.dot(xm[zz, rows, :], block, preferred_element_type=F32)
                    total = term if total is None else total + term
                if first:
                    acc[j, :, lanes] = total
                else:
                    acc[j, :, lanes] += total
                return 0

            lax.fori_loop(0, 9, body, 0)

        def attend(first_head, heads):
            def body(h, _):
                lanes = pl.ds(pl.multiple_of(h * HD, HD), HD)
                att[:, lanes] = attend_head(
                    acc[0, :, lanes], acc[1, :, lanes], acc[2, :, lanes], stk[:, lanes], stv[:, lanes], marks[0]
                )
                return 0

            lax.fori_loop(first_head, first_head + heads, body, 0)

        def block(zz):
            value = nt_dot(att[:, 0:OA], woa[zz].reshape(SUP, OA))
            return value + nt_dot(att[:, OA:CW], wob[zz].reshape(SUP, OB))

        def reduce_and_finish():
            ours = Summed(links, 0, block)
            ours.far()
            ours.near()
            ours.relay()
            ours.term(0)
            ours.wait()
            finish(ours, None)

        whole[0].wait()
        pl.semaphore_wait(gate_sem, 1)
        qkv.ya_own()
        qkv.zb_own(1)
        qkv.zb_own(-1)
        whole[1].wait()
        whole[2].wait()
        out.ya_own()
        qkv.yb_own(0)
        out.zb_own(1)
        out.zb_own(-1)
        modulations()
        out.yb_own(0)
        qkv.ya_relay(1)
        qkv.ya_relay(-1)
        out.ya_relay(1)
        out.ya_relay(-1)
        qkv.zb_relay(1, 1)
        qkv.zb_relay(-1, 1)
        qkv.yb_own(-1)
        out.zb_relay(1, 1)
        out.zb_relay(-1, 1)
        qkv.yb_own(1)
        qkv.za_own(0)
        qkv.za_own(1)
        qkv.yb_relay(0, 1)
        qkv.yb_relay(0, -1)
        qkv.zb_relay(1, 2)
        qkv.zb_relay(-1, 2)
        qkv.yb_own(-2)
        qkv.za_relay(1, 1, 0)
        qkv.za_relay(-1, 1, 0)
        qkv.yb_relay(-1, 1)
        qkv.yb_relay(-1, -1)
        qkv.yb_relay(1, 1)
        qkv.yb_relay(1, -1)
        qkv.za_relay(1, 1, 1)
        qkv.za_relay(-1, 1, 1)
        qkv.yb_own(2)
        qkv.zb_relay(1, 3)
        qkv.zb_relay(-1, 3)
        qkv.yb_relay(-2, 1)
        qkv.yb_relay(-2, -1)
        out.za_own(0)
        qkv.yb_own(-3)
        qkv.za_relay(1, 2, 0)
        qkv.za_relay(-1, 2, 0)
        qkv.yb_own(3)
        qkv.za_relay(1, 2, 1)
        qkv.za_relay(-1, 2, 1)
        qkv.yb_relay(2, 1)
        qkv.yb_relay(2, -1)
        qkv.yb_own(4)
        out.za_own(1)
        x_start()
        out.zb_relay(1, 2)
        out.zb_relay(-1, 2)
        qkv.za_relay(1, 3, 0)
        out.za_relay(-1, 1, 0)
        qkv.yb_relay(-3, 1)
        qkv.yb_relay(-3, -1)
        qkv.yb_relay(3, 1)
        qkv.yb_relay(3, -1)
        qkv.za_relay(-1, 3, 1)
        out.za_relay(1, 1, 0)
        x_relay(1)
        x_relay(-1)
        out.yb_relay(0, 1)
        out.yb_relay(0, -1)
        out.yb_own(-1)
        out.yb_own(1)
        out.yb_own(-2)
        out.za_relay(1, 1, 1)
        out.zb_relay(-1, 3)
        out.yb_own(2)
        out.za_relay(-1, 1, 1)
        qkv.yb_relay(4, 1)
        qkv.yb_relay(4, -1)
        x_fin()
        layer_norm(0, 1)
        out.zb_relay(1, 3)
        out.yb_own(-3)
        out.za_relay(-1, 2, 0)
        layer_norm(1, 1)
        out.yb_own(3)
        layer_norm(2, 1)
        layer_norm(3, 1)
        qkv.fin(0)
        qkv.fin(-1)
        qkv.fin(1)
        project((0, -1, 1), True)
        out.yb_relay(-1, 1)
        out.yb_relay(-1, -1)
        out.yb_relay(1, 1)
        out.yb_relay(1, -1)
        out.yb_relay(-2, 1)
        out.yb_relay(-2, -1)
        out.yb_relay(2, 1)
        out.yb_relay(2, -1)
        out.za_relay(1, 2, 0)
        qkv.fin(-2)
        qkv.fin(2)
        project((-2, 2), False)
        out.yb_relay(-3, 1)
        out.yb_relay(-3, -1)
        out.yb_own(4)
        out.yb_relay(3, 1)
        out.yb_relay(3, -1)
        out.za_relay(1, 2, 1)
        out.za_relay(-1, 2, 1)
        qkv.fin(-3)
        qkv.fin(3)
        project((-3, 3), False)
        qkv.fin(4)
        project((4,), False)
        out.yb_relay(4, 1)
        out.yb_relay(4, -1)
        out.za_relay(1, 3, 0)
        whole[3].wait()
        whole[4].wait()
        attend(0, 1)
        attend(1, 1)
        out.za_relay(-1, 3, 1)
        attend(2, 1)
        attend(3, 1)
        attend(4, 1)
        attend(5, 1)
        out.fin(0)
        out.fin(-1)
        out.fin(1)
        out.fin(-2)
        out.fin(2)
        out.fin(-3)
        out.fin(3)
        out.fin(4)
        reduce_and_finish()
        result_ref[...] = res[...]
        for copy in links.started:
            copy.wait_send()


def shards(
    hidden_in, patch_ends, timestep, mod_weight, qkv_weight, out_weight, stale_keys, stale_values
):
    feats = jnp.broadcast_to(embed_time(timestep), (16, FREQ))
    marks = jnp.broadcast_to(jnp.pad(patch_ends, ((0, 0), (0, HD - patch_ends.shape[1]))), (8, HD))
    mod_mat = jnp.swapaxes(mod_weight[0], 0, 1)
    qkv_mat = jnp.swapaxes(qkv_weight[0], 0, 1)
    out_mat = jnp.swapaxes(out_weight[0], 0, 1)
    anywhere = pl.BlockSpec(memory_space=pl.ANY)
    vmem = pl.BlockSpec(memory_space=pltpu.VMEM)
    half = CW // 2
    result = pl.pallas_call(
        kernel,
        out_shape=jax.ShapeDtypeStruct((SLOT, CW), BF16),
        in_specs=[pl.BlockSpec(memory_space=pltpu.SMEM), vmem, vmem] + [anywhere] * 6,
        out_specs=vmem,
        scratch_shapes=[
            pltpu.VMEM((3, NZ, NY, KB, CW), BF16),
            pltpu.VMEM((NZ, NY, KB, OA), BF16),
            pltpu.VMEM((NZ, NY, KB, OB), BF16),
            pltpu.VMEM((3, FREQ, NX * CW), BF16),
            pltpu.VMEM((2, 3, 16, NX * CW), F32),
            pltpu.VMEM((2, NX, SLOT, CW), BF16),
            pltpu.VMEM((NZ, 2 * SLOT, SUP), BF16),
            pltpu.VMEM((3, SLOT, CW), F32),
            pltpu.VMEM((3, 2 * SLOT, half), F32),
            pltpu.VMEM((SLOT, CW), BF16),
            pltpu.VMEM((SLOT, CW), BF16),
            pltpu.VMEM((2, SLOT, half), BF16),
            pltpu.VMEM((2, SLOT, half), BF16),
            pltpu.VMEM((SLOT, CW), BF16),
            pltpu.VMEM((2 * SLOT, half), BF16),
            pltpu.VMEM((NX, 2 * SLOT, CW), BF16),
            pltpu.VMEM((2 * SLOT, CW), F32),
            pltpu.VMEM((3, 2 * SLOT, CW), BF16),
            pltpu.VMEM((SLOT, CW), BF16),
            pltpu.VMEM((16, FREQ), BF16),
            pltpu.VMEM((2, 8, HD), jnp.int32),
            pltpu.VMEM((SLOT, CW), BF16),
            pltpu.SemaphoreType.DMA((N_SEM,)),
            pltpu.SemaphoreType.DMA((N_SEM,)),
            pltpu.SemaphoreType.DMA((8,)),
            pltpu.SemaphoreType.DMA((2,)),
            pltpu.SemaphoreType.REGULAR,
        ],
        compiler_params=pltpu.CompilerParams(
            collective_id=0, has_side_effects=True, vmem_limit_bytes=62 * 1024 * 1024
        ),
        name="patch_layers",
    )(
        patch_ends, feats, marks, hidden_in[0], mod_mat, qkv_mat, out_mat,
        stale_keys[0, 0], stale_values[0, 0],
    )
    return result[None, None]


def solution(mesh):
    return jax.shard_map(
        shards,
        mesh=mesh,
        in_specs=(
            P("row", None, "col"),
            P("row", None),
            P("row"),
            P("section", None, None, None),
            P("section", "row", None, "col"),
            P("section", "col", "row"),
            P("section", "row", None, "col"),
            P("section", "row", None, "col"),
        ),
        out_specs=P("section", "row", None, "col"),
        check_vma=False,
    )
```

```python
import functools
import math

import jax
import jax.numpy as jnp
from jax import lax
from jax.experimental import pallas as pl
from jax.experimental.pallas import tpu as pltpu
from jax.sharding import PartitionSpec as P

HD = 128
FREQ = 256
NX, NY, NZ = 4, 4, 8
KB = 96
CW = 768
SUP = NY * KB
SLOT = 256
HEADS = CW // HD
OA = 512
OB = CW - OA
OA2, OB2 = OA // 2, OB // 2
MESH = pl.DeviceIdType.MESH
F32 = jnp.float32
BF16 = jnp.bfloat16
N_SEM = 160


def embed_time(timestep):
    half_width = FREQ // 2
    frequency = jnp.exp(
        jnp.arange(half_width, dtype=F32) * (-math.log(10000.0) / half_width)
    )
    angles = timestep.astype(F32)[:, None] * frequency[None, :]
    return jnp.concatenate([jnp.cos(angles), jnp.sin(angles)], axis=1).astype(BF16)


class Links:
    def __init__(self, send_sem, recv_sem):
        self.send_sem, self.recv_sem = send_sem, recv_sem
        self.count = 0
        self.started = []

    def slot(self):
        self.count += 1
        return self.count - 1

    def copy(self, index, source, target, device):
        return pltpu.make_async_remote_copy(
            src_ref=source, dst_ref=target, send_sem=self.send_sem.at[index],
            recv_sem=self.recv_sem.at[index], device_id=device, device_id_type=MESH,
        )

    def start(self, out_view, in_view, device, target=None):
        index = self.slot()
        outgoing = self.copy(index, out_view, out_view if target is None else target, device)
        outgoing.start()
        self.started.append(outgoing)
        return self.copy(index, in_view, in_view, device)


class Gather:
    def __init__(self, links, pos, devs, views):
        self.links, self.devs = links, devs
        self.y, self.z = pos
        self.a_shard, self.a_half, self.a_sup, self.b_shard, self.b_half = views
        self.inc = {}

    def zi(self, off):
        return lax.rem(self.z + (off + NZ), NZ)

    def yi(self, off):
        return lax.rem(self.y + (off + NY), NY)

    def go(self, key, out_view, in_view, device):
        self.inc[key] = self.links.start(out_view, in_view, self.devs[device])

    def wait(self, *key):
        self.inc.pop(key).wait_recv()

    def dev(self, axis, sign):
        return axis + ("+" if sign == 1 else "-")

    def ya_own(self):
        for sign in (1, -1):
            self.go(("ya", sign), self.a_shard(self.z, self.y), self.a_shard(self.z, self.yi(-sign)), self.dev("y", sign))

    def ya_relay(self, sign):
        half = 0 if sign == 1 else 1
        self.wait("ya", sign)
        self.go(("yah", sign), self.a_half(self.z, self.yi(-sign), half), self.a_half(self.z, self.yi(-2 * sign), half), self.dev("y", sign))

    def zb_own(self, sign):
        self.zb_send(sign, 0)

    def zb_relay(self, sign, d):
        self.wait("zb", sign, d - 1)
        self.zb_send(sign, d)

    def zb_send(self, sign, d):
        here, there = self.zi(-sign * d), self.zi(-sign * (d + 1))
        if d < NZ // 2 - 1:
            views = self.b_shard(here, self.y), self.b_shard(there, self.y)
        else:
            half = 0 if sign == 1 else 1
            views = self.b_half(here, self.y, half), self.b_half(there, self.y, half)
        self.go(("zb", sign, d), *views, self.dev("z", sign))

    def yb_own(self, off):
        if off == NZ // 2:
            for sign in (1, -1):
                self.wait("zb", sign, off - 1)
        for sign in (1, -1):
            self.go(("yb", off, sign), self.b_shard(self.zi(off), self.y), self.b_shard(self.zi(off), self.yi(-sign)), self.dev("y", sign))

    def yb_relay(self, off, sign):
        half = 0 if sign == 1 else 1
        self.wait("yb", off, sign)
        self.go(("ybh", off, sign), self.b_half(self.zi(off), self.yi(-sign), half), self.b_half(self.zi(off), self.yi(-2 * sign), half), self.dev("y", sign))

    def za_own(self, half):
        if half == 0:
            for sign in (1, -1):
                self.wait("yah", sign)
        for sign in (1, -1):
            self.za_send(sign, 0, half)

    def za_relay(self, sign, d, half):
        self.wait("za", sign, d - 1, half)
        self.za_send(sign, d, half)

    def za_send(self, sign, d, half):
        here, there = self.zi(-sign * d), self.zi(-sign * (d + 1))
        self.go(("za", sign, d, half), self.a_sup(here, half), self.a_sup(there, half), self.dev("z", sign))

    def fin(self, off):
        for sign in (1, -1):
            self.wait("ybh", off, sign)
        for key in [k for k in self.inc if k[0] == "za" and -k[1] * (k[2] + 1) % NZ == off % NZ]:
            self.wait(*key)


class PairGather:
    def __init__(self, links, pos, devs, views):
        self.links, self.devs = links, devs
        self.y, self.z = pos
        self.mate_y = NY - 1 - self.y
        self.near_y = self.y + 1 - 2 * lax.rem(self.y, 2)
        self.source, self.landing, self.a_slot, self.a_sup, self.b_slot = views
        self.inc = {}

    def zi(self, off):
        return lax.rem(self.z + (off + NZ), NZ)

    def slot(self, k):
        return self.y if k == 0 else self.mate_y

    def near_slot(self, k):
        return self.near_y if k == 0 else NY - 1 - self.near_y

    def go(self, key, out_view, in_view, device, target=None):
        self.inc[key] = self.links.start(out_view, in_view, self.devs[device], target)

    def wait(self, *key):
        self.inc.pop(key).wait_recv()

    def inject(self):
        for i, (source, target) in enumerate(zip(self.source, self.landing(self.y))):
            self.go(("inj", i), source, self.landing(self.mate_y)[i], "pair", target)

    def injected(self):
        for i in range(len(self.source)):
            if ("inj", i) in self.inc:
                self.wait("inj", i)

    def ya_own(self, k):
        if k == 1:
            self.injected()
        self.go(("ya", k), self.a_slot(self.z, self.slot(k)), self.a_slot(self.z, self.near_slot(k)), "near")

    def za_own(self, half):
        if half == 0:
            for k in range(2):
                self.wait("ya", k)
        for sign in (1, -1):
            self.za_send(sign, 0, half)

    def za_relay(self, sign, d, half):
        self.wait("za", sign, d - 1, half)
        self.za_send(sign, d, half)

    def za_send(self, sign, d, half):
        here, there = self.zi(-sign * d), self.zi(-sign * (d + 1))
        self.go(("za", sign, d, half), self.a_sup(here, half), self.a_sup(there, half), "z+" if sign == 1 else "z-")

    def zb_own(self, k, sign):
        if k == 1:
            self.injected()
        self.zb_send(k, sign, 0)

    def zb_relay(self, k, sign, d):
        self.wait("zb", k, sign, d - 1)
        self.zb_send(k, sign, d)

    def zb_send(self, k, sign, d):
        here, there = self.zi(-sign * d), self.zi(-sign * (d + 1))
        self.go(("zb", k, sign, d), self.b_slot(here, self.slot(k)), self.b_slot(there, self.slot(k)), "z+" if sign == 1 else "z-")

    def yb_own(self, off, k):
        if off == 0 and k == 1:
            self.injected()
        for sign in (1, -1):
            for d in range(NZ // 2):
                if off % NZ == -sign * (d + 1) % NZ and ("zb", k, sign, d) in self.inc:
                    self.wait("zb", k, sign, d)
        self.go(("yb", off, k), self.b_slot(self.zi(off), self.slot(k)), self.b_slot(self.zi(off), self.near_slot(k)), "near")

    def fin(self, off):
        for k in range(2):
            self.wait("yb", off, k)
        self.fin_a(off)

    def fin_a(self, off):
        for key in [k for k in self.inc if k[0] == "za" and -k[1] * (k[2] + 1) % NZ == off % NZ]:
            self.wait(*key)


def nt_dot(left, right):
    return lax.dot_general(left, right, (((1,), (1,)), ((), ())), preferred_element_type=F32)


def pairs_dot(lefts, rights):
    total = None
    for i in range(0, len(lefts), 2):
        left = jnp.concatenate(lefts[i:i + 2], axis=1)
        right = jnp.concatenate(rights[i:i + 2], axis=0)
        term = jnp.dot(left, right, preferred_element_type=F32)
        total = term if total is None else total + term
    return total


def kernel(
    ends_ref, feats_ref, marks_ref, hidden_hbm, mod_hbm, qkv_hbm, out_hbm, keys_hbm, values_hbm,
    result_ref,
    wbuf, woa, wob, modw, modv, xbuf, xm, acc, acc2, stk, stv, stk2, stv2, att, att2, part, own_part, rs_in, pair_in,
    feats_in, marks, res,
    send_sem, recv_sem, local_sem, hand_sem, gate_sem,
):
    s = lax.axis_index("section")
    row = lax.axis_index("row")
    x = lax.axis_index("col")
    z, y = row // NY, lax.rem(row, NY)

    def zy(zz, yy):
        return lax.rem(zz + NZ, NZ) * NY + lax.rem(yy + NY, NY)

    def xi(off):
        return lax.rem(x + (off + NX), NX)

    devs = {
        "y+": (s, zy(z, y + 1), x), "y-": (s, zy(z, y - 1), x),
        "z+": (s, zy(z + 1, y), x), "z-": (s, zy(z - 1, y), x),
        "x+": (s, row, xi(1)), "x-": (s, row, xi(-1)),
        "mate": (1 - s, row, x),
    }
    load_mod = pltpu.make_async_copy(mod_hbm, modw, local_sem.at[3])
    load_mod.start()
    load_x = pltpu.make_async_copy(hidden_hbm, xbuf.at[0, x], local_sem.at[6])
    half_lanes = CW // 2
    group = y // 2
    mine = pl.ds(pl.multiple_of(group * half_lanes, half_lanes), half_lanes)
    other = pl.ds(pl.multiple_of((1 - group) * half_lanes, half_lanes), half_lanes)

    def out_lanes(which, size, start):
        return pl.ds(pl.multiple_of(which * half_lanes + start, HD), size)

    whole = [
        pltpu.make_async_copy(qkv_hbm, wbuf.at[:, z, y], local_sem.at[0]),
        pltpu.make_async_copy(out_hbm.at[:, pl.ds(0, OA)], woa.at[z, y], local_sem.at[1]),
        pltpu.make_async_copy(out_hbm.at[:, pl.ds(OA, OB)], wob.at[z, y], local_sem.at[2]),
        pltpu.make_async_copy(keys_hbm, stk, local_sem.at[4]),
        pltpu.make_async_copy(values_hbm, stv, local_sem.at[5]),
    ]
    halves = [
        pltpu.make_async_copy(qkv_hbm.at[:, :, mine], wbuf.at[:, z, y, :, pl.ds(0, half_lanes)], local_sem.at[0]),
        pltpu.make_async_copy(out_hbm.at[:, out_lanes(group, OA2, 0)], woa.at[z, y, :, pl.ds(0, OA2)], local_sem.at[1]),
        pltpu.make_async_copy(out_hbm.at[:, out_lanes(group, OB2, OA2)], wob.at[z, y, :, pl.ds(0, OB2)], local_sem.at[2]),
        pltpu.make_async_copy(keys_hbm.at[:, mine], stk2.at[0], local_sem.at[4]),
        pltpu.make_async_copy(values_hbm.at[:, mine], stv2.at[0], local_sem.at[5]),
    ]

    @pl.when(s == 0)
    def _():
        for copy in halves:
            copy.start()
        load_x.start()

    @pl.when(s == 1)
    def _():
        for copy in whole:
            copy.start()

    marks[0] = marks_ref[...]

    barrier = pltpu.get_barrier_semaphore()
    for device in devs.values():
        pl.semaphore_signal(barrier, inc=1, device_id=device, device_id_type=MESH)
    pl.semaphore_wait(barrier, len(devs))

    handed = pltpu.make_async_remote_copy(
        src_ref=res, dst_ref=xbuf.at[0, x], send_sem=hand_sem.at[0], recv_sem=hand_sem.at[1],
        device_id=devs["mate"], device_id_type=MESH,
    )

    def modulation(r, feats):
        def body(j, _):
            modv[r, j] = jnp.dot(feats[...], modw[j], preferred_element_type=F32)
            return 0

        lax.fori_loop(0, 3, body, 0)

    def layer_norm(first, count):
        width = NX * CW

        def body(i, _):
            r = first * 64 // SLOT
            rows = pl.ds(pl.multiple_of(i * 16 - r * SLOT, 16), 16)
            to_rows = pl.ds(pl.multiple_of(i * 16, 16), 16)
            parts = [xbuf[r, c, rows, :].astype(F32) for c in range(NX)]
            total = sum(jnp.sum(p, axis=-1, keepdims=True) for p in parts)
            squares = sum(jnp.sum(p * p, axis=-1, keepdims=True) for p in parts)
            mean = total / width
            var = squares / width - mean * mean
            inv = 1.0 / jnp.sqrt(var + 1e-06)
            for b in range(NZ):
                lanes = pl.ds(b * SUP, SUP)
                piece = parts[b // 2][:, (b % 2) * SUP:(b % 2 + 1) * SUP]
                normed = (piece - mean) * inv
                xm[b, to_rows, :] = (normed * (1.0 + modv[r, 1, 0:1, lanes]) + modv[r, 0, 0:1, lanes]).astype(BF16)
            return 0

        lax.fori_loop(first * 4, (first + count) * 4, body, 0)

    def attend_head(q, k, v, old_k, old_v, mark):
        e0, e1, e2, e3 = (mark[0:1, m:m + 1] for m in range(4))
        q_pos = lax.broadcasted_iota(jnp.int32, (SLOT, 1), 0)
        limit = jnp.where(q_pos < e0, e0, jnp.where(q_pos < e1, e1, jnp.where(q_pos < e2, e2, e3)))
        k_pos = lax.broadcasted_iota(jnp.int32, (SLOT, SLOT), 1)
        fresh = k_pos < limit
        ok = k_pos < e3

        def norm(raw):
            return (raw * (1.0 / jnp.sqrt(jnp.mean(raw * raw, axis=-1, keepdims=True) + 1e-06))).astype(BF16)

        q, k, v = norm(q), norm(k), v.astype(BF16)
        scores = jnp.where(fresh, nt_dot(q, k), nt_dot(q, old_k)) * (1.0 / math.sqrt(HD))
        weights = jnp.where(ok, jnp.exp(scores), 0.0)
        weights = weights * (1.0 / jnp.sum(weights, axis=-1, keepdims=True))
        new_part = jnp.where(fresh, weights, 0.0).astype(BF16)
        old_part = jnp.where(fresh, 0.0, weights).astype(BF16)
        mixed = jnp.dot(new_part, v, preferred_element_type=F32) + jnp.dot(
            old_part, old_v, preferred_element_type=F32
        )
        return mixed.astype(BF16)

    e3 = ends_ref[0, 3]
    half_rows = SLOT // 2
    lanes_own = pl.ds(pl.multiple_of(x * CW, CW), CW)

    class Summed:
        def __init__(self, links, base, block):
            self.links, self.base, self.block = links, base, block
            self.low, self.high = pl.ds(base, half_rows), pl.ds(base + half_rows, half_rows)
            self.ways = ((1, "x+", self.low, self.high, 1), (-1, "x-", self.high, self.low, 3))
            self.opp, self.tail = {}, []

        def rows(self):
            return pl.ds(self.base, SLOT)

        def term(self, off):
            for i in range(2):
                value = self.block(2 * xi(off) + i)
                if off == 0:
                    own_part[self.rows(), i * SUP:(i + 1) * SUP] = value
                else:
                    part[off, self.rows(), i * SUP:(i + 1) * SUP] = value.astype(BF16)

        def far(self):
            self.term(2)
            for sign, dev, rows, _, _ in self.ways:
                self.opp[sign] = self.links.start(part.at[2, rows], rs_in.at[0, rows], devs[dev], rs_in.at[0, rows])

        def near(self):
            self.term(1)
            self.term(3)
            for sign, dev, _, others, slot in self.ways:
                land = rs_in.at[1 if sign == 1 else 2, others]
                self.tail.append(self.links.start(part.at[slot, others], land, devs[dev], land))

        def relay(self):
            for sign, dev, rows, _, slot in self.ways:
                self.opp[sign].wait_recv()
                part[slot, rows, :] = (part[slot, rows, :].astype(F32) + rs_in[0, rows, :].astype(F32)).astype(BF16)
                land = rs_in.at[1 if sign == 1 else 2, rows]
                self.tail.append(self.links.start(part.at[slot, rows], land, devs[dev], land))

        def wait(self):
            for incoming in self.tail:
                incoming.wait_recv()

        def total(self, i):
            rows = pl.ds(pl.multiple_of(self.base + i * 16, 16), 16)
            return own_part[rows, :] + rs_in[1, rows, :].astype(F32) + rs_in[2, rows, :].astype(F32)

    def finish(summed, extra):
        def body(i, _):
            rows = pl.ds(pl.multiple_of(i * 16, 16), 16)
            branch = summed.total(i)
            if extra is not None:
                branch += extra[rows, :].astype(F32)
            updated = xbuf[0, x, rows, :].astype(F32) + modv[0, 2, 0:1, lanes_own] * branch
            pos = lax.broadcasted_iota(jnp.int32, (16, 1), 0) + i * 16
            res[rows, :] = jnp.where(pos < e3, updated, 0.0).astype(BF16)
            return 0

        lax.fori_loop(0, SLOT // 16, body, 0)

    def share_x(links, r, inc):
        def own():
            for sign, dev in ((1, "x+"), (-1, "x-")):
                inc["x", r, sign] = links.start(xbuf.at[r, x], xbuf.at[r, xi(-sign)], devs[dev])

        def relay(sign):
            rows = pl.ds(0 if sign == 1 else half_rows, half_rows)
            inc["x", r, sign].wait_recv()
            inc["xh", r, sign] = links.start(
                xbuf.at[r, xi(-sign), rows], xbuf.at[r, xi(-2 * sign), rows], devs["x+" if sign == 1 else "x-"]
            )

        def fin():
            for sign in (1, -1):
                inc["xh", r, sign].wait_recv()

        return own, relay, fin

    def open_gate():
        pl.semaphore_signal(gate_sem, inc=1, device_id=devs["mate"], device_id_type=MESH)

    @pl.when(s == 0)
    def _():
        links = Links(send_sem, recv_sem)
        mate_y = NY - 1 - y
        near_y = y + 1 - 2 * lax.rem(y, 2)
        ways = dict(devs)
        ways["pair"] = (s, z * NY + mate_y, x)
        ways["near"] = (s, z * NY + near_y, x)
        low = pl.ds(0, half_lanes)
        qkv = PairGather(links, (y, z), ways, (
            [qkv_hbm.at[:, :, other]],
            lambda yy: [wbuf.at[:, z, yy, :, low]],
            lambda zz, yy: wbuf.at[0, zz, yy, :, low],
            lambda zz, h: wbuf.at[0, zz, pl.ds(2 * h, 2), :, low],
            lambda zz, yy: wbuf.at[pl.ds(1, 2), zz, yy, :, low],
        ))
        a_low, b_low = pl.ds(0, OA2), pl.ds(0, OB2)
        out = PairGather(links, (y, z), ways, (
            [out_hbm.at[:, out_lanes(1 - group, OA2, 0)], out_hbm.at[:, out_lanes(1 - group, OB2, OA2)]],
            lambda yy: [woa.at[z, yy, :, a_low], wob.at[z, yy, :, b_low]],
            lambda zz, yy: woa.at[zz, yy, :, a_low],
            lambda zz, h: woa.at[zz, pl.ds(2 * h, 2), :, a_low],
            lambda zz, yy: wob.at[zz, yy, :, b_low],
        ))
        inc = {}
        shares = [share_x(links, r, inc) for r in range(2)]

        def send_small():
            inc["f"] = links.start(feats_ref, feats_in, ways["pair"], feats_in)
            inc["m"] = links.start(marks_ref, marks.at[1], ways["pair"], marks.at[1])

        def send_hidden():
            inc["xc"] = links.start(hidden_hbm, xbuf.at[1, x], ways["pair"], xbuf.at[1, x])

        def send_stale():
            inc["sk"] = links.start(keys_hbm.at[:, other], stk2.at[1], ways["pair"], stk2.at[1])
            inc["sv"] = links.start(values_hbm.at[:, other], stv2.at[1], ways["pair"], stv2.at[1])

        def x_own(r):
            if r == 0:
                load_x.wait()
            else:
                inc["xc"].wait_recv()
            shares[r][0]()

        def x_relay(r, sign):
            shares[r][1](sign)

        def modulations():
            load_mod.wait()
            modulation(0, feats_ref)
            inc["f"].wait_recv()
            modulation(1, feats_in)

        def project(offs, first):
            def body(t, _):
                j = t // 2
                rows = pl.ds(pl.multiple_of(lax.rem(t, 2) * SLOT, SLOT), SLOT)
                total = pairs_dot(
                    [xm[qkv.zi(off), rows, :] for off in offs],
                    [wbuf[j, qkv.zi(off), :, :, low].reshape(SUP, half_lanes) for off in offs],
                )
                if first:
                    acc2[j, rows, :] = total
                else:
                    acc2[j, rows, :] += total
                return 0

            lax.fori_loop(0, 6, body, 0)

        def attend(first_item, items):
            def body(t, _):
                r = t // 3
                rows = pl.ds(pl.multiple_of(r * SLOT, SLOT), SLOT)
                lanes = pl.ds(pl.multiple_of(lax.rem(t, 3) * HD, HD), HD)
                att2[rows, lanes] = attend_head(
                    acc2[0, rows, lanes], acc2[1, rows, lanes], acc2[2, rows, lanes],
                    stk2[r, :, lanes], stv2[r, :, lanes], marks[r],
                )
                return 0

            lax.fori_loop(first_item, first_item + items, body, 0)

        def block_of(base):
            rows = pl.ds(base, SLOT)

            def block(zz):
                value = nt_dot(att2[rows, 0:OA2], woa[zz, :, :, a_low].reshape(SUP, OA2))
                return value + nt_dot(att2[rows, OA2:OA2 + OB2], wob[zz, :, :, b_low].reshape(SUP, OB2))

            return block

        def reduce_and_finish():
            theirs, ours = Summed(links, SLOT, block_of(SLOT)), Summed(links, 0, block_of(0))
            theirs.far()
            theirs.near()
            theirs.relay()
            ours.far()
            ours.near()
            theirs.term(0)
            theirs.wait()

            def body(i, _):
                att_rows = pl.ds(pl.multiple_of(i * 16, 16), 16)
                part[0, att_rows, :] = theirs.total(i).astype(BF16)
                return 0

            lax.fori_loop(0, SLOT // 16, body, 0)
            paired = links.start(part.at[0, pl.ds(0, SLOT)], pair_in, ways["pair"], pair_in)
            ours.relay()
            ours.term(0)
            ours.wait()
            paired.wait_recv()
            finish(ours, pair_in)

        halves[0].wait()
        send_small()
        qkv.inject()
        send_hidden()
        out.inject()
        send_stale()
        qkv.ya_own(0)
        qkv.zb_own(0, 1)
        qkv.zb_own(0, -1)
        halves[1].wait()
        halves[2].wait()
        out.ya_own(0)
        qkv.yb_own(0, 0)
        out.zb_own(0, 1)
        out.zb_own(0, -1)
        out.yb_own(0, 0)
        x_own(0)
        modulations()
        qkv.zb_relay(0, 1, 1)
        qkv.zb_relay(0, -1, 1)
        qkv.yb_own(-1, 0)
        qkv.yb_own(1, 0)
        out.zb_relay(0, 1, 1)
        out.zb_relay(0, -1, 1)
        out.yb_own(-1, 0)
        out.yb_own(1, 0)
        qkv.ya_own(1)
        qkv.zb_own(1, 1)
        qkv.zb_own(1, -1)
        qkv.yb_own(0, 1)
        x_relay(0, 1)
        x_relay(0, -1)
        qkv.zb_relay(0, 1, 2)
        qkv.zb_relay(0, -1, 2)
        qkv.yb_own(-2, 0)
        out.zb_relay(0, 1, 2)
        out.zb_relay(0, -1, 2)
        qkv.yb_own(2, 0)
        x_own(1)
        qkv.zb_relay(1, 1, 1)
        qkv.zb_relay(1, -1, 1)
        qkv.yb_own(-1, 1)
        out.zb_own(1, 1)
        out.zb_own(1, -1)
        qkv.za_own(0)
        qkv.za_own(1)
        shares[0][2]()
        layer_norm(0, 1)
        qkv.zb_relay(0, 1, 3)
        layer_norm(1, 1)
        out.ya_own(1)
        qkv.yb_own(-3, 0)
        layer_norm(2, 1)
        out.zb_relay(0, 1, 3)
        layer_norm(3, 1)
        qkv.zb_relay(1, 1, 2)
        qkv.zb_relay(1, -1, 2)
        out.zb_relay(1, -1, 1)
        qkv.yb_own(3, 0)
        out.zb_relay(1, 1, 1)
        qkv.za_relay(1, 1, 0)
        qkv.za_relay(-1, 1, 0)
        qkv.yb_own(1, 1)
        x_relay(1, 1)
        x_relay(1, -1)
        qkv.za_relay(1, 1, 1)
        qkv.za_relay(-1, 1, 1)
        qkv.yb_own(-2, 1)
        out.za_own(0)
        qkv.zb_relay(1, -1, 3)
        qkv.yb_own(4, 0)
        out.zb_relay(1, -1, 2)
        out.za_own(1)
        shares[1][2]()
        layer_norm(4, 1)
        layer_norm(5, 1)
        qkv.yb_own(2, 1)
        qkv.za_relay(-1, 2, 0)
        out.zb_relay(1, 1, 2)
        layer_norm(6, 1)
        layer_norm(7, 1)
        qkv.fin(0)
        qkv.fin(-1)
        project((0, -1), True)
        qkv.yb_own(-3, 1)
        qkv.za_relay(1, 2, 0)
        qkv.za_relay(-1, 2, 1)
        qkv.za_relay(1, 2, 1)
        out.za_relay(-1, 1, 0)
        qkv.yb_own(3, 1)
        qkv.fin(1)
        qkv.fin(-2)
        project((1, -2), False)
        qkv.yb_own(4, 1)
        out.zb_relay(1, -1, 3)
        out.za_relay(1, 1, 0)
        out.za_relay(1, 1, 1)
        out.za_relay(-1, 1, 1)
        out.yb_own(-2, 0)
        out.yb_own(2, 0)
        out.yb_own(-3, 0)
        qkv.za_relay(1, 3, 0)
        out.yb_own(3, 0)
        out.yb_own(4, 0)
        out.yb_own(0, 1)
        out.yb_own(-1, 1)
        out.yb_own(1, 1)
        qkv.za_relay(-1, 3, 1)
        out.yb_own(-2, 1)
        qkv.fin(2)
        qkv.fin(-3)
        project((2, -3), False)
        out.yb_own(2, 1)
        out.yb_own(-3, 1)
        out.yb_own(3, 1)
        out.yb_own(4, 1)
        out.za_relay(-1, 2, 0)
        out.za_relay(1, 2, 0)
        out.za_relay(1, 2, 1)
        out.za_relay(-1, 2, 1)
        open_gate()
        qkv.fin(3)
        qkv.fin(4)
        project((3, 4), False)
        out.za_relay(1, 3, 0)
        halves[3].wait()
        halves[4].wait()
        inc["sk"].wait_recv()
        inc["sv"].wait_recv()
        inc["m"].wait_recv()
        attend(0, 1)
        attend(1, 1)
        out.za_relay(-1, 3, 1)
        attend(2, 1)
        attend(3, 1)
        attend(4, 1)
        attend(5, 1)
        out.fin(0)
        out.fin(-1)
        out.fin(1)
        out.fin(-2)
        out.fin(2)
        out.fin(-3)
        out.fin(3)
        out.fin(4)
        reduce_and_finish()
        handed.start()
        result_ref[...] = res[...]
        handed.wait_send()
        for copy in links.started:
            copy.wait_send()

    @pl.when(s == 1)
    def _():
        links = Links(send_sem, recv_sem)
        qkv = Gather(links, (y, z), devs, (
            lambda zz, yy: wbuf.at[0, zz, yy],
            lambda zz, yy, h: wbuf.at[0, zz, yy, pl.ds(h * (KB // 2), KB // 2)],
            lambda zz, h: wbuf.at[0, zz, pl.ds(2 * h, 2)],
            lambda zz, yy: wbuf.at[pl.ds(1, 2), zz, yy],
            lambda zz, yy, h: wbuf.at[1 + h, zz, yy],
        ))
        out = Gather(links, (y, z), devs, (
            lambda zz, yy: woa.at[zz, yy],
            lambda zz, yy, h: woa.at[zz, yy, pl.ds(h * (KB // 2), KB // 2)],
            lambda zz, h: woa.at[zz, pl.ds(2 * h, 2)],
            lambda zz, yy: wob.at[zz, yy],
            lambda zz, yy, h: wob.at[zz, yy, pl.ds(h * (KB // 2), KB // 2)],
        ))
        inc = {}
        share = share_x(links, 0, inc)

        def x_start():
            handed.wait_recv()
            share[0]()

        def x_relay(sign):
            share[1](sign)

        def x_fin():
            share[2]()

        def modulations():
            load_mod.wait()
            modulation(0, feats_ref)

        rows = pl.ds(0, SLOT)

        def project(offs, first):
            def body(t, _):
                j = t // 3
                lanes = pl.ds(pl.multiple_of(lax.rem(t, 3) * 256, 256), 256)
                total = pairs_dot(
                    [xm[qkv.zi(off), rows, :] for off in offs],
                    [wbuf[j, qkv.zi(off), :, :, lanes].reshape(SUP, 256) for off in offs],
                )
                if first:
                    acc[j, :, lanes] = total
                else:
                    acc[j, :, lanes] += total
                return 0

            lax.fori_loop(0, 9, body, 0)

        def attend(first_head, heads):
            def body(h, _):
                lanes = pl.ds(pl.multiple_of(h * HD, HD), HD)
                att[:, lanes] = attend_head(
                    acc[0, :, lanes], acc[1, :, lanes], acc[2, :, lanes], stk[:, lanes], stv[:, lanes], marks[0]
                )
                return 0

            lax.fori_loop(first_head, first_head + heads, body, 0)

        def block(zz):
            value = nt_dot(att[:, 0:OA], woa[zz].reshape(SUP, OA))
            return value + nt_dot(att[:, OA:CW], wob[zz].reshape(SUP, OB))

        def reduce_and_finish():
            ours = Summed(links, 0, block)
            ours.far()
            ours.near()
            ours.relay()
            ours.term(0)
            ours.wait()
            finish(ours, None)

        whole[0].wait()
        pl.semaphore_wait(gate_sem, 1)
        qkv.ya_own()
        qkv.zb_own(1)
        qkv.zb_own(-1)
        whole[1].wait()
        whole[2].wait()
        out.ya_own()
        qkv.yb_own(0)
        out.zb_own(1)
        out.zb_own(-1)
        out.yb_own(0)
        modulations()
        qkv.ya_relay(1)
        qkv.ya_relay(-1)
        out.ya_relay(1)
        out.ya_relay(-1)
        qkv.zb_relay(1, 1)
        qkv.zb_relay(-1, 1)
        qkv.yb_own(-1)
        qkv.yb_own(1)
        out.zb_relay(1, 1)
        out.zb_relay(-1, 1)
        out.yb_own(-1)
        out.yb_own(1)
        qkv.yb_relay(0, 1)
        qkv.yb_relay(0, -1)
        qkv.za_own(0)
        qkv.za_own(1)
        out.za_own(0)
        out.yb_relay(0, 1)
        out.yb_relay(0, -1)
        qkv.zb_relay(1, 2)
        qkv.zb_relay(-1, 2)
        qkv.yb_own(-2)
        qkv.yb_relay(-1, 1)
        qkv.yb_relay(-1, -1)
        out.za_own(1)
        qkv.yb_own(2)
        qkv.za_relay(1, 1, 0)
        qkv.za_relay(-1, 1, 0)
        qkv.yb_relay(1, 1)
        qkv.yb_relay(1, -1)
        qkv.za_relay(1, 1, 1)
        qkv.za_relay(-1, 1, 1)
        out.yb_relay(-1, 1)
        out.yb_relay(-1, -1)
        out.yb_relay(1, 1)
        out.yb_relay(1, -1)
        out.zb_relay(1, 2)
        out.zb_relay(-1, 2)
        out.yb_own(-2)
        out.yb_own(2)
        qkv.yb_relay(-2, 1)
        qkv.yb_relay(-2, -1)
        qkv.zb_relay(1, 3)
        qkv.zb_relay(-1, 3)
        qkv.yb_own(-3)
        out.za_relay(1, 1, 0)
        out.za_relay(-1, 1, 0)
        qkv.yb_own(3)
        out.za_relay(1, 1, 1)
        out.za_relay(-1, 1, 1)
        qkv.za_relay(1, 2, 0)
        qkv.za_relay(-1, 2, 0)
        qkv.yb_relay(2, 1)
        qkv.yb_relay(2, -1)
        out.yb_relay(-2, 1)
        out.yb_relay(-2, -1)
        out.yb_relay(2, 1)
        out.yb_relay(2, -1)
        qkv.za_relay(1, 2, 1)
        x_start()
        qkv.za_relay(-1, 2, 1)
        qkv.yb_own(4)
        out.zb_relay(1, 3)
        out.zb_relay(-1, 3)
        out.yb_own(-3)
        qkv.yb_relay(-3, 1)
        qkv.yb_relay(-3, -1)
        out.za_relay(1, 2, 0)
        out.za_relay(-1, 2, 0)
        out.yb_own(3)
        out.za_relay(1, 2, 1)
        out.za_relay(-1, 2, 1)
        x_relay(1)
        x_relay(-1)
        qkv.yb_relay(3, 1)
        qkv.yb_relay(3, -1)
        qkv.za_relay(1, 3, 0)
        x_fin()
        layer_norm(0, 1)
        layer_norm(1, 1)
        layer_norm(2, 1)
        layer_norm(3, 1)
        qkv.yb_relay(4, 1)
        qkv.yb_relay(4, -1)
        qkv.za_relay(-1, 3, 1)
        qkv.fin(0)
        qkv.fin(-1)
        qkv.fin(1)
        qkv.fin(-2)
        project((0, -1, 1, -2), True)
        out.yb_relay(-3, 1)
        out.yb_relay(-3, -1)
        out.yb_relay(3, 1)
        out.yb_relay(3, -1)
        out.yb_own(4)
        out.za_relay(1, 3, 0)
        qkv.fin(2)
        qkv.fin(-3)
        project((2, -3), False)
        out.za_relay(-1, 3, 1)
        out.yb_relay(4, 1)
        out.yb_relay(4, -1)
        qkv.fin(3)
        qkv.fin(4)
        project((3, 4), False)
        whole[3].wait()
        whole[4].wait()
        attend(0, 1)
        attend(1, 1)
        attend(2, 1)
        attend(3, 1)
        attend(4, 1)
        attend(5, 1)
        out.fin(0)
        out.fin(-1)
        out.fin(1)
        out.fin(-2)
        out.fin(2)
        out.fin(-3)
        out.fin(3)
        out.fin(4)
        reduce_and_finish()
        result_ref[...] = res[...]
        for copy in links.started:
            copy.wait_send()


def shards(
    hidden_in, patch_ends, timestep, mod_weight, qkv_weight, out_weight, stale_keys, stale_values
):
    feats = jnp.broadcast_to(embed_time(timestep), (16, FREQ))
    marks = jnp.broadcast_to(jnp.pad(patch_ends, ((0, 0), (0, HD - patch_ends.shape[1]))), (8, HD))
    mod_mat = jnp.swapaxes(mod_weight[0], 0, 1)
    qkv_mat = jnp.swapaxes(qkv_weight[0], 0, 1)
    out_mat = jnp.swapaxes(out_weight[0], 0, 1)
    anywhere = pl.BlockSpec(memory_space=pl.ANY)
    vmem = pl.BlockSpec(memory_space=pltpu.VMEM)
    half = CW // 2
    result = pl.pallas_call(
        kernel,
        out_shape=jax.ShapeDtypeStruct((SLOT, CW), BF16),
        in_specs=[pl.BlockSpec(memory_space=pltpu.SMEM), vmem, vmem] + [anywhere] * 6,
        out_specs=vmem,
        scratch_shapes=[
            pltpu.VMEM((3, NZ, NY, KB, CW), BF16),
            pltpu.VMEM((NZ, NY, KB, OA), BF16),
            pltpu.VMEM((NZ, NY, KB, OB), BF16),
            pltpu.VMEM((3, FREQ, NX * CW), BF16),
            pltpu.VMEM((2, 3, 16, NX * CW), F32),
            pltpu.VMEM((2, NX, SLOT, CW), BF16),
            pltpu.VMEM((NZ, 2 * SLOT, SUP), BF16),
            pltpu.VMEM((3, SLOT, CW), F32),
            pltpu.VMEM((3, 2 * SLOT, half), F32),
            pltpu.VMEM((SLOT, CW), BF16),
            pltpu.VMEM((SLOT, CW), BF16),
            pltpu.VMEM((2, SLOT, half), BF16),
            pltpu.VMEM((2, SLOT, half), BF16),
            pltpu.VMEM((SLOT, CW), BF16),
            pltpu.VMEM((2 * SLOT, half), BF16),
            pltpu.VMEM((NX, 2 * SLOT, CW), BF16),
            pltpu.VMEM((2 * SLOT, CW), F32),
            pltpu.VMEM((3, 2 * SLOT, CW), BF16),
            pltpu.VMEM((SLOT, CW), BF16),
            pltpu.VMEM((16, FREQ), BF16),
            pltpu.VMEM((2, 8, HD), jnp.int32),
            pltpu.VMEM((SLOT, CW), BF16),
            pltpu.SemaphoreType.DMA((N_SEM,)),
            pltpu.SemaphoreType.DMA((N_SEM,)),
            pltpu.SemaphoreType.DMA((8,)),
            pltpu.SemaphoreType.DMA((2,)),
            pltpu.SemaphoreType.REGULAR,
        ],
        compiler_params=pltpu.CompilerParams(
            collective_id=0, has_side_effects=True, vmem_limit_bytes=62 * 1024 * 1024
        ),
        name="patch_layers",
    )(
        patch_ends, feats, marks, hidden_in[0], mod_mat, qkv_mat, out_mat,
        stale_keys[0, 0], stale_values[0, 0],
    )
    return result[None, None]


def solution(mesh):
    return jax.shard_map(
        shards,
        mesh=mesh,
        in_specs=(
            P("row", None, "col"),
            P("row", None),
            P("row"),
            P("section", None, None, None),
            P("section", "row", None, "col"),
            P("section", "col", "row"),
            P("section", "row", None, "col"),
            P("section", "row", None, "col"),
        ),
        out_specs=P("section", "row", None, "col"),
        check_vma=False,
    )
```

```python
import functools
import math

import jax
import jax.numpy as jnp
from jax import lax
from jax.experimental import pallas as pl
from jax.experimental.pallas import tpu as pltpu
from jax.sharding import PartitionSpec as P

HD = 128
FREQ = 256
NX, NY, NZ = 4, 4, 8
KB = 96
CW = 768
SUP = NY * KB
SLOT = 256
HEADS = CW // HD
OA = 512
OB = CW - OA
OA2, OB2 = OA // 2, OB // 2
MESH = pl.DeviceIdType.MESH
F32 = jnp.float32
BF16 = jnp.bfloat16
N_SEM = 176


def embed_time(timestep):
    half_width = FREQ // 2
    frequency = jnp.exp(
        jnp.arange(half_width, dtype=F32) * (-math.log(10000.0) / half_width)
    )
    angles = timestep.astype(F32)[:, None] * frequency[None, :]
    return jnp.concatenate([jnp.cos(angles), jnp.sin(angles)], axis=1).astype(BF16)


class Links:
    def __init__(self, send_sem, recv_sem):
        self.send_sem, self.recv_sem = send_sem, recv_sem
        self.count = 0
        self.started = []

    def slot(self):
        self.count += 1
        return self.count - 1

    def copy(self, index, source, target, device):
        return pltpu.make_async_remote_copy(
            src_ref=source, dst_ref=target, send_sem=self.send_sem.at[index],
            recv_sem=self.recv_sem.at[index], device_id=device, device_id_type=MESH,
        )

    def start(self, out_view, in_view, device, target=None):
        index = self.slot()
        outgoing = self.copy(index, out_view, out_view if target is None else target, device)
        outgoing.start()
        self.started.append(outgoing)
        return self.copy(index, in_view, in_view, device)


class Gather:
    def __init__(self, links, pos, devs, views):
        self.links, self.devs = links, devs
        self.y, self.z = pos
        self.a_shard, self.a_half, self.a_sup, self.b_shard, self.b_half = views
        self.inc = {}

    def zi(self, off):
        return lax.rem(self.z + (off + NZ), NZ)

    def yi(self, off):
        return lax.rem(self.y + (off + NY), NY)

    def go(self, key, out_view, in_view, device):
        self.inc[key] = self.links.start(out_view, in_view, self.devs[device])

    def wait(self, *key):
        self.inc.pop(key).wait_recv()

    def dev(self, axis, sign):
        return axis + ("+" if sign == 1 else "-")

    def ya_own(self):
        for sign in (1, -1):
            self.go(("ya", sign), self.a_shard(self.z, self.y), self.a_shard(self.z, self.yi(-sign)), self.dev("y", sign))

    def ya_relay(self, sign):
        half = 0 if sign == 1 else 1
        self.wait("ya", sign)
        self.go(("yah", sign), self.a_half(self.z, self.yi(-sign), half), self.a_half(self.z, self.yi(-2 * sign), half), self.dev("y", sign))

    def zb_own(self, sign):
        self.zb_send(sign, 0)

    def zb_relay(self, sign, d):
        self.wait("zb", sign, d - 1)
        self.zb_send(sign, d)

    def zb_send(self, sign, d):
        here, there = self.zi(-sign * d), self.zi(-sign * (d + 1))
        if d < NZ // 2 - 1:
            views = self.b_shard(here, self.y), self.b_shard(there, self.y)
        else:
            half = 0 if sign == 1 else 1
            views = self.b_half(here, self.y, half), self.b_half(there, self.y, half)
        self.go(("zb", sign, d), *views, self.dev("z", sign))

    def yb_own(self, off):
        if off == NZ // 2:
            for sign in (1, -1):
                self.wait("zb", sign, off - 1)
        for sign in (1, -1):
            self.go(("yb", off, sign), self.b_shard(self.zi(off), self.y), self.b_shard(self.zi(off), self.yi(-sign)), self.dev("y", sign))

    def yb_relay(self, off, sign):
        half = 0 if sign == 1 else 1
        self.wait("yb", off, sign)
        self.go(("ybh", off, sign), self.b_half(self.zi(off), self.yi(-sign), half), self.b_half(self.zi(off), self.yi(-2 * sign), half), self.dev("y", sign))

    def za_own(self, half):
        if half == 0:
            for sign in (1, -1):
                self.wait("yah", sign)
        for sign in (1, -1):
            self.za_send(sign, 0, half)

    def za_relay(self, sign, d, half):
        self.wait("za", sign, d - 1, half)
        self.za_send(sign, d, half)

    def za_send(self, sign, d, half):
        here, there = self.zi(-sign * d), self.zi(-sign * (d + 1))
        self.go(("za", sign, d, half), self.a_sup(here, half), self.a_sup(there, half), self.dev("z", sign))

    def fin(self, off):
        for sign in (1, -1):
            self.wait("ybh", off, sign)
        for key in [k for k in self.inc if k[0] == "za" and -k[1] * (k[2] + 1) % NZ == off % NZ]:
            self.wait(*key)


class PairGather:
    def __init__(self, links, pos, devs, views):
        self.links, self.devs = links, devs
        self.y, self.z = pos
        self.mate_y = NY - 1 - self.y
        self.near_y = self.y + 1 - 2 * lax.rem(self.y, 2)
        self.source, self.landing, self.a_slot, self.a_sup, self.b_slot = views
        self.inc = {}

    def zi(self, off):
        return lax.rem(self.z + (off + NZ), NZ)

    def slot(self, k):
        return self.y if k == 0 else self.mate_y

    def near_slot(self, k):
        return self.near_y if k == 0 else NY - 1 - self.near_y

    def go(self, key, out_view, in_view, device, target=None):
        self.inc[key] = self.links.start(out_view, in_view, self.devs[device], target)

    def wait(self, *key):
        self.inc.pop(key).wait_recv()

    def inject(self):
        for i, (source, target) in enumerate(zip(self.source, self.landing(self.y))):
            self.go(("inj", i), source, self.landing(self.mate_y)[i], "pair", target)

    def injected(self):
        for i in range(len(self.source)):
            if ("inj", i) in self.inc:
                self.wait("inj", i)

    def ya_own(self, k):
        if k == 1:
            self.injected()
        self.go(("ya", k), self.a_slot(self.z, self.slot(k)), self.a_slot(self.z, self.near_slot(k)), "near")

    def za_own(self, half):
        if half == 0:
            for k in range(2):
                self.wait("ya", k)
        for sign in (1, -1):
            self.za_send(sign, 0, half)

    def za_relay(self, sign, d, half):
        self.wait("za", sign, d - 1, half)
        self.za_send(sign, d, half)

    def za_send(self, sign, d, half):
        here, there = self.zi(-sign * d), self.zi(-sign * (d + 1))
        self.go(("za", sign, d, half), self.a_sup(here, half), self.a_sup(there, half), "z+" if sign == 1 else "z-")

    def zb_own(self, k, sign):
        if k == 1:
            self.injected()
        self.zb_send(k, sign, 0)

    def zb_relay(self, k, sign, d):
        self.wait("zb", k, sign, d - 1)
        self.zb_send(k, sign, d)

    def zb_send(self, k, sign, d):
        here, there = self.zi(-sign * d), self.zi(-sign * (d + 1))
        self.go(("zb", k, sign, d), self.b_slot(here, self.slot(k)), self.b_slot(there, self.slot(k)), "z+" if sign == 1 else "z-")

    def yb_own(self, off, k):
        if off == 0 and k == 1:
            self.injected()
        for sign in (1, -1):
            for d in range(NZ // 2):
                if off % NZ == -sign * (d + 1) % NZ and ("zb", k, sign, d) in self.inc:
                    self.wait("zb", k, sign, d)
        self.go(("yb", off, k), self.b_slot(self.zi(off), self.slot(k)), self.b_slot(self.zi(off), self.near_slot(k)), "near")

    def fin(self, off):
        for k in range(2):
            self.wait("yb", off, k)
        self.fin_a(off)

    def fin_a(self, off):
        for key in [k for k in self.inc if k[0] == "za" and -k[1] * (k[2] + 1) % NZ == off % NZ]:
            self.wait(*key)


def nt_dot(left, right):
    return lax.dot_general(left, right, (((1,), (1,)), ((), ())), preferred_element_type=F32)


def pairs_dot(lefts, rights):
    total = None
    for i in range(0, len(lefts), 2):
        left = jnp.concatenate(lefts[i:i + 2], axis=1)
        right = jnp.concatenate(rights[i:i + 2], axis=0)
        term = jnp.dot(left, right, preferred_element_type=F32)
        total = term if total is None else total + term
    return total


def kernel(
    ends_ref, feats_ref, marks_ref, hidden_hbm, mod_hbm, qkv_hbm, out_hbm, keys_hbm, values_hbm,
    result_ref,
    wbuf, woa, wob, modw, modv, xbuf, xm, acc, acc2, stk, stv, stk2, stv2, att, att2, part, own_part, rs_in, pair_in,
    feats_in, marks, res,
    send_sem, recv_sem, local_sem, hand_sem, gate_sem,
):
    s = lax.axis_index("section")
    row = lax.axis_index("row")
    x = lax.axis_index("col")
    z, y = row // NY, lax.rem(row, NY)

    def zy(zz, yy):
        return lax.rem(zz + NZ, NZ) * NY + lax.rem(yy + NY, NY)

    def xi(off):
        return lax.rem(x + (off + NX), NX)

    devs = {
        "y+": (s, zy(z, y + 1), x), "y-": (s, zy(z, y - 1), x),
        "z+": (s, zy(z + 1, y), x), "z-": (s, zy(z - 1, y), x),
        "x+": (s, row, xi(1)), "x-": (s, row, xi(-1)),
        "mate": (1 - s, row, x),
    }
    load_mod = pltpu.make_async_copy(mod_hbm, modw, local_sem.at[3])
    load_mod.start()
    load_x = pltpu.make_async_copy(hidden_hbm, xbuf.at[0, x], local_sem.at[6])
    half_lanes = CW // 2
    group = y // 2
    mine = pl.ds(pl.multiple_of(group * half_lanes, half_lanes), half_lanes)
    other = pl.ds(pl.multiple_of((1 - group) * half_lanes, half_lanes), half_lanes)

    def out_lanes(which, size, start):
        return pl.ds(pl.multiple_of(which * half_lanes + start, HD), size)

    whole = [
        pltpu.make_async_copy(qkv_hbm, wbuf.at[:, z, y], local_sem.at[0]),
        pltpu.make_async_copy(out_hbm.at[:, pl.ds(0, OA)], woa.at[z, y], local_sem.at[1]),
        pltpu.make_async_copy(out_hbm.at[:, pl.ds(OA, OB)], wob.at[z, y], local_sem.at[2]),
        pltpu.make_async_copy(keys_hbm, stk, local_sem.at[4]),
        pltpu.make_async_copy(values_hbm, stv, local_sem.at[5]),
    ]
    halves = [
        pltpu.make_async_copy(qkv_hbm.at[:, :, mine], wbuf.at[:, z, y, :, pl.ds(0, half_lanes)], local_sem.at[0]),
        pltpu.make_async_copy(out_hbm.at[:, out_lanes(group, OA2, 0)], woa.at[z, y, :, pl.ds(0, OA2)], local_sem.at[1]),
        pltpu.make_async_copy(out_hbm.at[:, out_lanes(group, OB2, OA2)], wob.at[z, y, :, pl.ds(0, OB2)], local_sem.at[2]),
        pltpu.make_async_copy(keys_hbm.at[:, mine], stk2.at[0], local_sem.at[4]),
        pltpu.make_async_copy(values_hbm.at[:, mine], stv2.at[0], local_sem.at[5]),
    ]

    @pl.when(s == 0)
    def _():
        for copy in halves:
            copy.start()
        load_x.start()

    @pl.when(s == 1)
    def _():
        for copy in whole:
            copy.start()

    marks[0] = marks_ref[...]

    barrier = pltpu.get_barrier_semaphore()
    for device in devs.values():
        pl.semaphore_signal(barrier, inc=1, device_id=device, device_id_type=MESH)
    pl.semaphore_wait(barrier, len(devs))

    handed = pltpu.make_async_remote_copy(
        src_ref=res, dst_ref=xbuf.at[0, x], send_sem=hand_sem.at[0], recv_sem=hand_sem.at[1],
        device_id=devs["mate"], device_id_type=MESH,
    )

    def modulation(r, feats):
        def body(j, _):
            modv[r, j] = jnp.dot(feats[...], modw[j], preferred_element_type=F32)
            return 0

        lax.fori_loop(0, 3, body, 0)

    def layer_norm(first, count):
        width = NX * CW

        def body(i, _):
            r = first * 64 // SLOT
            rows = pl.ds(pl.multiple_of(i * 16 - r * SLOT, 16), 16)
            to_rows = pl.ds(pl.multiple_of(i * 16, 16), 16)
            parts = [xbuf[r, c, rows, :].astype(F32) for c in range(NX)]
            total = sum(jnp.sum(p, axis=-1, keepdims=True) for p in parts)
            squares = sum(jnp.sum(p * p, axis=-1, keepdims=True) for p in parts)
            mean = total / width
            var = squares / width - mean * mean
            inv = 1.0 / jnp.sqrt(var + 1e-06)
            for b in range(NZ):
                lanes = pl.ds(b * SUP, SUP)
                piece = parts[b // 2][:, (b % 2) * SUP:(b % 2 + 1) * SUP]
                normed = (piece - mean) * inv
                xm[b, to_rows, :] = (normed * (1.0 + modv[r, 1, 0:1, lanes]) + modv[r, 0, 0:1, lanes]).astype(BF16)
            return 0

        lax.fori_loop(first * 4, (first + count) * 4, body, 0)

    def attend_head(q, k, v, old_k, old_v, mark):
        e0, e1, e2, e3 = (mark[0:1, m:m + 1] for m in range(4))
        q_pos = lax.broadcasted_iota(jnp.int32, (SLOT, 1), 0)
        limit = jnp.where(q_pos < e0, e0, jnp.where(q_pos < e1, e1, jnp.where(q_pos < e2, e2, e3)))
        k_pos = lax.broadcasted_iota(jnp.int32, (SLOT, SLOT), 1)
        fresh = k_pos < limit
        ok = k_pos < e3

        def norm(raw):
            return (raw * (1.0 / jnp.sqrt(jnp.mean(raw * raw, axis=-1, keepdims=True) + 1e-06))).astype(BF16)

        q, k, v = norm(q), norm(k), v.astype(BF16)
        scores = jnp.where(fresh, nt_dot(q, k), nt_dot(q, old_k)) * (1.0 / math.sqrt(HD))
        weights = jnp.where(ok, jnp.exp(scores), 0.0)
        weights = weights * (1.0 / jnp.sum(weights, axis=-1, keepdims=True))
        new_part = jnp.where(fresh, weights, 0.0).astype(BF16)
        old_part = jnp.where(fresh, 0.0, weights).astype(BF16)
        mixed = jnp.dot(new_part, v, preferred_element_type=F32) + jnp.dot(
            old_part, old_v, preferred_element_type=F32
        )
        return mixed.astype(BF16)

    e3 = ends_ref[0, 3]
    half_rows = SLOT // 2
    lanes_own = pl.ds(pl.multiple_of(x * CW, CW), CW)

    class Summed:
        def __init__(self, links, base, block):
            self.links, self.base, self.block = links, base, block
            self.low, self.high = pl.ds(base, half_rows), pl.ds(base + half_rows, half_rows)
            self.ways = ((1, "x+", self.low, self.high, 1), (-1, "x-", self.high, self.low, 3))
            self.opp, self.tail = {}, []

        def rows(self):
            return pl.ds(self.base, SLOT)

        def term(self, off):
            for i in range(2):
                value = self.block(2 * xi(off) + i)
                if off == 0:
                    own_part[self.rows(), i * SUP:(i + 1) * SUP] = value
                else:
                    part[off, self.rows(), i * SUP:(i + 1) * SUP] = value.astype(BF16)

        def far(self):
            self.term(2)
            for sign, dev, rows, _, _ in self.ways:
                self.opp[sign] = self.links.start(part.at[2, rows], rs_in.at[0, rows], devs[dev], rs_in.at[0, rows])

        def near(self):
            self.term(1)
            self.term(3)
            for sign, dev, _, others, slot in self.ways:
                land = rs_in.at[1 if sign == 1 else 2, others]
                self.tail.append(self.links.start(part.at[slot, others], land, devs[dev], land))

        def relay(self):
            for sign, dev, rows, _, slot in self.ways:
                self.opp[sign].wait_recv()
                part[slot, rows, :] = (part[slot, rows, :].astype(F32) + rs_in[0, rows, :].astype(F32)).astype(BF16)
                land = rs_in.at[1 if sign == 1 else 2, rows]
                self.tail.append(self.links.start(part.at[slot, rows], land, devs[dev], land))

        def wait(self):
            for incoming in self.tail:
                incoming.wait_recv()

        def total(self, i):
            rows = pl.ds(pl.multiple_of(self.base + i * 16, 16), 16)
            return own_part[rows, :] + rs_in[1, rows, :].astype(F32) + rs_in[2, rows, :].astype(F32)

    def finish(summed, extra, target):
        def body(i, _):
            rows = pl.ds(pl.multiple_of(i * 16, 16), 16)
            branch = summed.total(i)
            if extra is not None:
                branch += extra[rows, :].astype(F32)
            updated = xbuf[0, x, rows, :].astype(F32) + modv[0, 2, 0:1, lanes_own] * branch
            pos = lax.broadcasted_iota(jnp.int32, (16, 1), 0) + i * 16
            target[rows, :] = jnp.where(pos < e3, updated, 0.0).astype(BF16)
            return 0

        lax.fori_loop(0, SLOT // 16, body, 0)

    def share_x(links, r, inc):
        rows_of = pl.ds(0, half_rows), pl.ds(half_rows, half_rows)
        ways = ((1, "x+", 0), (-1, "x-", 1))

        def own():
            for step in range(2):
                for sign, dev, half in ways:
                    rows = rows_of[half if step == 0 else 1 - half]
                    inc["x", r, sign, step] = links.start(xbuf.at[r, x, rows], xbuf.at[r, xi(-sign), rows], devs[dev])

        def relay(sign):
            half = 0 if sign == 1 else 1
            rows = rows_of[half]
            inc["x", r, sign, 0].wait_recv()
            inc["xh", r, sign] = links.start(
                xbuf.at[r, xi(-sign), rows], xbuf.at[r, xi(-2 * sign), rows], devs["x+" if sign == 1 else "x-"]
            )

        def fin():
            for sign in (1, -1):
                inc["x", r, sign, 1].wait_recv()
                inc["xh", r, sign].wait_recv()

        return own, relay, fin

    def open_gate():
        pl.semaphore_signal(gate_sem, inc=1, device_id=devs["mate"], device_id_type=MESH)

    @pl.when(s == 0)
    def _():
        links = Links(send_sem, recv_sem)
        mate_y = NY - 1 - y
        near_y = y + 1 - 2 * lax.rem(y, 2)
        ways = dict(devs)
        ways["pair"] = (s, z * NY + mate_y, x)
        ways["near"] = (s, z * NY + near_y, x)
        low = pl.ds(0, half_lanes)
        qkv = PairGather(links, (y, z), ways, (
            [qkv_hbm.at[:, :, other]],
            lambda yy: [wbuf.at[:, z, yy, :, low]],
            lambda zz, yy: wbuf.at[0, zz, yy, :, low],
            lambda zz, h: wbuf.at[0, zz, pl.ds(2 * h, 2), :, low],
            lambda zz, yy: wbuf.at[pl.ds(1, 2), zz, yy, :, low],
        ))
        a_low, b_low = pl.ds(0, OA2), pl.ds(0, OB2)
        out = PairGather(links, (y, z), ways, (
            [out_hbm.at[:, out_lanes(1 - group, OA2, 0)], out_hbm.at[:, out_lanes(1 - group, OB2, OA2)]],
            lambda yy: [woa.at[z, yy, :, a_low], wob.at[z, yy, :, b_low]],
            lambda zz, yy: woa.at[zz, yy, :, a_low],
            lambda zz, h: woa.at[zz, pl.ds(2 * h, 2), :, a_low],
            lambda zz, yy: wob.at[zz, yy, :, b_low],
        ))
        inc = {}
        shares = [share_x(links, r, inc) for r in range(2)]

        def send_small():
            inc["f"] = links.start(feats_ref, feats_in, ways["pair"], feats_in)
            inc["m"] = links.start(marks_ref, marks.at[1], ways["pair"], marks.at[1])

        def send_hidden():
            inc["xc"] = links.start(hidden_hbm, xbuf.at[1, x], ways["pair"], xbuf.at[1, x])

        def send_stale():
            inc["sk"] = links.start(keys_hbm.at[:, other], stk2.at[1], ways["pair"], stk2.at[1])
            inc["sv"] = links.start(values_hbm.at[:, other], stv2.at[1], ways["pair"], stv2.at[1])

        def x_own(r):
            if r == 0:
                load_x.wait()
            else:
                inc["xc"].wait_recv()
            shares[r][0]()

        def x_relay(r, sign):
            shares[r][1](sign)

        def modulations():
            load_mod.wait()
            modulation(0, feats_ref)
            inc["f"].wait_recv()
            modulation(1, feats_in)

        def project(offs, first):
            def body(t, _):
                j = t // 2
                rows = pl.ds(pl.multiple_of(lax.rem(t, 2) * SLOT, SLOT), SLOT)
                total = pairs_dot(
                    [xm[qkv.zi(off), rows, :] for off in offs],
                    [wbuf[j, qkv.zi(off), :, :, low].reshape(SUP, half_lanes) for off in offs],
                )
                if first:
                    acc2[j, rows, :] = total
                else:
                    acc2[j, rows, :] += total
                return 0

            lax.fori_loop(0, 6, body, 0)

        def attend(first_item, items):
            def body(t, _):
                r = t // 3
                rows = pl.ds(pl.multiple_of(r * SLOT, SLOT), SLOT)
                lanes = pl.ds(pl.multiple_of(lax.rem(t, 3) * HD, HD), HD)
                att2[rows, lanes] = attend_head(
                    acc2[0, rows, lanes], acc2[1, rows, lanes], acc2[2, rows, lanes],
                    stk2[r, :, lanes], stv2[r, :, lanes], marks[r],
                )
                return 0

            lax.fori_loop(first_item, first_item + items, body, 0)

        def block_of(base):
            rows = pl.ds(base, SLOT)

            def block(zz):
                value = nt_dot(att2[rows, 0:OA2], woa[zz, :, :, a_low].reshape(SUP, OA2))
                return value + nt_dot(att2[rows, OA2:OA2 + OB2], wob[zz, :, :, b_low].reshape(SUP, OB2))

            return block

        def reduce_and_finish():
            theirs, ours = Summed(links, SLOT, block_of(SLOT)), Summed(links, 0, block_of(0))
            theirs.far()
            theirs.near()
            theirs.relay()
            ours.far()
            ours.near()
            theirs.term(0)
            theirs.wait()

            def body(i, _):
                att_rows = pl.ds(pl.multiple_of(i * 16, 16), 16)
                part[0, att_rows, :] = theirs.total(i).astype(BF16)
                return 0

            lax.fori_loop(0, SLOT // 16, body, 0)
            paired = links.start(part.at[0, pl.ds(0, SLOT)], pair_in, ways["pair"], pair_in)
            ours.relay()
            ours.term(0)
            ours.wait()
            paired.wait_recv()
            finish(ours, pair_in, res)

        halves[0].wait()
        send_small()
        qkv.inject()
        send_hidden()
        out.inject()
        send_stale()
        qkv.ya_own(0)
        qkv.zb_own(0, 1)
        qkv.zb_own(0, -1)
        halves[1].wait()
        halves[2].wait()
        out.ya_own(0)
        qkv.yb_own(0, 0)
        out.zb_own(0, 1)
        out.zb_own(0, -1)
        out.yb_own(0, 0)
        x_own(0)
        modulations()
        qkv.zb_relay(0, 1, 1)
        qkv.zb_relay(0, -1, 1)
        qkv.yb_own(-1, 0)
        qkv.yb_own(1, 0)
        out.zb_relay(0, 1, 1)
        out.zb_relay(0, -1, 1)
        out.yb_own(-1, 0)
        out.yb_own(1, 0)
        x_relay(0, 1)
        x_relay(0, -1)
        qkv.ya_own(1)
        qkv.zb_own(1, 1)
        qkv.zb_own(1, -1)
        qkv.yb_own(0, 1)
        qkv.zb_relay(0, 1, 2)
        qkv.zb_relay(0, -1, 2)
        qkv.yb_own(-2, 0)
        out.zb_relay(0, 1, 2)
        out.zb_relay(0, -1, 2)
        qkv.yb_own(2, 0)
        shares[0][2]()
        layer_norm(0, 1)
        x_own(1)
        qkv.zb_relay(1, 1, 1)
        qkv.zb_relay(1, -1, 1)
        layer_norm(1, 1)
        out.ya_own(1)
        qkv.yb_own(-1, 1)
        qkv.za_own(0)
        qkv.za_own(1)
        layer_norm(2, 1)
        qkv.zb_relay(0, 1, 3)
        out.zb_own(1, -1)
        layer_norm(3, 1)
        qkv.yb_own(-3, 0)
        out.zb_own(1, 1)
        out.zb_relay(0, 1, 3)
        qkv.zb_relay(1, 1, 2)
        qkv.zb_relay(1, -1, 2)
        x_relay(1, 1)
        x_relay(1, -1)
        qkv.yb_own(3, 0)
        qkv.za_relay(1, 1, 0)
        qkv.za_relay(-1, 1, 0)
        qkv.yb_own(1, 1)
        out.za_own(0)
        qkv.za_relay(-1, 1, 1)
        qkv.yb_own(-2, 1)
        out.zb_relay(1, -1, 1)
        qkv.za_relay(1, 1, 1)
        shares[1][2]()
        layer_norm(4, 1)
        qkv.zb_relay(1, -1, 3)
        qkv.yb_own(4, 0)
        layer_norm(5, 1)
        out.za_own(1)
        layer_norm(6, 1)
        layer_norm(7, 1)
        qkv.yb_own(2, 1)
        qkv.za_relay(-1, 2, 0)
        out.zb_relay(1, 1, 1)
        qkv.fin(0)
        qkv.fin(-1)
        project((0, -1), True)
        qkv.yb_own(-3, 1)
        qkv.za_relay(1, 2, 0)
        out.za_relay(-1, 1, 0)
        out.za_relay(1, 1, 0)
        qkv.za_relay(-1, 2, 1)
        qkv.yb_own(3, 1)
        qkv.za_relay(1, 2, 1)
        out.zb_relay(1, -1, 2)
        qkv.fin(1)
        qkv.fin(-2)
        project((1, -2), False)
        qkv.yb_own(4, 1)
        out.zb_relay(1, 1, 2)
        out.za_relay(1, 1, 1)
        out.za_relay(-1, 1, 1)
        out.yb_own(-2, 0)
        out.yb_own(2, 0)
        out.yb_own(-3, 0)
        qkv.za_relay(1, 3, 0)
        out.yb_own(3, 0)
        out.yb_own(4, 0)
        out.yb_own(0, 1)
        out.yb_own(-1, 1)
        out.za_relay(-1, 2, 0)
        out.za_relay(1, 2, 0)
        out.yb_own(1, 1)
        out.yb_own(-2, 1)
        out.yb_own(2, 1)
        qkv.za_relay(-1, 3, 1)
        qkv.fin(2)
        qkv.fin(-3)
        project((2, -3), False)
        out.zb_relay(1, -1, 3)
        out.yb_own(3, 1)
        out.yb_own(-3, 1)
        out.za_relay(-1, 2, 1)
        out.za_relay(1, 2, 1)
        open_gate()
        qkv.fin(3)
        qkv.fin(4)
        project((3, 4), False)
        out.yb_own(4, 1)
        out.za_relay(1, 3, 0)
        halves[3].wait()
        halves[4].wait()
        inc["sk"].wait_recv()
        inc["sv"].wait_recv()
        inc["m"].wait_recv()
        attend(0, 1)
        out.za_relay(-1, 3, 1)
        attend(1, 1)
        attend(2, 1)
        attend(3, 1)
        attend(4, 1)
        attend(5, 1)
        out.fin(0)
        out.fin(-1)
        out.fin(1)
        out.fin(-2)
        out.fin(2)
        out.fin(-3)
        out.fin(3)
        out.fin(4)
        reduce_and_finish()
        handed.start()
        result_ref[...] = res[...]
        handed.wait_send()
        for copy in links.started:
            copy.wait_send()

    @pl.when(s == 1)
    def _():
        links = Links(send_sem, recv_sem)
        qkv = Gather(links, (y, z), devs, (
            lambda zz, yy: wbuf.at[0, zz, yy],
            lambda zz, yy, h: wbuf.at[0, zz, yy, pl.ds(h * (KB // 2), KB // 2)],
            lambda zz, h: wbuf.at[0, zz, pl.ds(2 * h, 2)],
            lambda zz, yy: wbuf.at[pl.ds(1, 2), zz, yy],
            lambda zz, yy, h: wbuf.at[1 + h, zz, yy],
        ))
        out = Gather(links, (y, z), devs, (
            lambda zz, yy: woa.at[zz, yy],
            lambda zz, yy, h: woa.at[zz, yy, pl.ds(h * (KB // 2), KB // 2)],
            lambda zz, h: woa.at[zz, pl.ds(2 * h, 2)],
            lambda zz, yy: wob.at[zz, yy],
            lambda zz, yy, h: wob.at[zz, yy, pl.ds(h * (KB // 2), KB // 2)],
        ))
        inc = {}
        share = share_x(links, 0, inc)

        def x_start():
            handed.wait_recv()
            share[0]()

        def x_relay(sign):
            share[1](sign)

        def x_fin():
            share[2]()

        def modulations():
            load_mod.wait()
            modulation(0, feats_ref)

        rows = pl.ds(0, SLOT)

        def project(offs, first):
            def body(t, _):
                j = t // 3
                lanes = pl.ds(pl.multiple_of(lax.rem(t, 3) * 256, 256), 256)
                total = pairs_dot(
                    [xm[qkv.zi(off), rows, :] for off in offs],
                    [wbuf[j, qkv.zi(off), :, :, lanes].reshape(SUP, 256) for off in offs],
                )
                if first:
                    acc[j, :, lanes] = total
                else:
                    acc[j, :, lanes] += total
                return 0

            lax.fori_loop(0, 9, body, 0)

        def attend(first_head, heads):
            def body(h, _):
                lanes = pl.ds(pl.multiple_of(h * HD, HD), HD)
                att[:, lanes] = attend_head(
                    acc[0, :, lanes], acc[1, :, lanes], acc[2, :, lanes], stk[:, lanes], stv[:, lanes], marks[0]
                )
                return 0

            lax.fori_loop(first_head, first_head + heads, body, 0)

        def block(zz):
            value = nt_dot(att[:, 0:OA], woa[zz].reshape(SUP, OA))
            return value + nt_dot(att[:, OA:CW], wob[zz].reshape(SUP, OB))

        def reduce_and_finish():
            ours = Summed(links, 0, block)
            ours.far()
            ours.near()
            ours.relay()
            ours.term(0)
            ours.wait()
            finish(ours, None, result_ref)

        whole[0].wait()
        pl.semaphore_wait(gate_sem, 1)
        qkv.ya_own()
        qkv.zb_own(1)
        qkv.zb_own(-1)
        whole[1].wait()
        whole[2].wait()
        out.ya_own()
        qkv.yb_own(0)
        out.zb_own(1)
        out.zb_own(-1)
        out.yb_own(0)
        modulations()
        qkv.ya_relay(1)
        qkv.ya_relay(-1)
        out.ya_relay(1)
        out.ya_relay(-1)
        qkv.zb_relay(1, 1)
        qkv.zb_relay(-1, 1)
        qkv.yb_own(-1)
        qkv.yb_own(1)
        out.zb_relay(1, 1)
        out.zb_relay(-1, 1)
        out.yb_own(-1)
        out.yb_own(1)
        qkv.yb_relay(0, 1)
        qkv.yb_relay(0, -1)
        qkv.za_own(0)
        qkv.za_own(1)
        out.za_own(0)
        out.yb_relay(0, 1)
        out.yb_relay(0, -1)
        qkv.zb_relay(1, 2)
        qkv.zb_relay(-1, 2)
        qkv.yb_own(-2)
        qkv.yb_relay(-1, 1)
        qkv.yb_relay(-1, -1)
        out.za_own(1)
        qkv.yb_own(2)
        qkv.za_relay(1, 1, 0)
        qkv.za_relay(-1, 1, 0)
        qkv.yb_relay(1, 1)
        qkv.yb_relay(1, -1)
        qkv.za_relay(1, 1, 1)
        qkv.za_relay(-1, 1, 1)
        out.yb_relay(-1, 1)
        out.yb_relay(-1, -1)
        out.yb_relay(1, 1)
        out.yb_relay(1, -1)
        out.zb_relay(1, 2)
        out.zb_relay(-1, 2)
        out.yb_own(-2)
        out.yb_own(2)
        qkv.yb_relay(-2, 1)
        qkv.yb_relay(-2, -1)
        qkv.zb_relay(1, 3)
        qkv.zb_relay(-1, 3)
        qkv.yb_own(-3)
        out.za_relay(1, 1, 0)
        out.za_relay(-1, 1, 0)
        qkv.yb_own(3)
        out.za_relay(1, 1, 1)
        out.za_relay(-1, 1, 1)
        qkv.za_relay(1, 2, 0)
        qkv.za_relay(-1, 2, 0)
        qkv.yb_relay(2, 1)
        qkv.yb_relay(2, -1)
        out.yb_relay(-2, 1)
        out.yb_relay(-2, -1)
        out.yb_relay(2, 1)
        out.yb_relay(2, -1)
        qkv.za_relay(1, 2, 1)
        x_start()
        qkv.za_relay(-1, 2, 1)
        qkv.yb_own(4)
        out.zb_relay(1, 3)
        out.zb_relay(-1, 3)
        out.yb_own(-3)
        qkv.yb_relay(-3, 1)
        qkv.yb_relay(-3, -1)
        out.za_relay(1, 2, 0)
        out.za_relay(-1, 2, 0)
        x_relay(1)
        x_relay(-1)
        out.yb_own(3)
        out.za_relay(1, 2, 1)
        out.za_relay(-1, 2, 1)
        qkv.yb_relay(3, 1)
        qkv.yb_relay(3, -1)
        x_fin()
        layer_norm(0, 1)
        layer_norm(1, 1)
        qkv.za_relay(1, 3, 0)
        layer_norm(2, 1)
        layer_norm(3, 1)
        qkv.fin(0)
        qkv.fin(-1)
        qkv.fin(1)
        qkv.fin(-2)
        project((0, -1, 1, -2), True)
        qkv.yb_relay(4, 1)
        qkv.yb_relay(4, -1)
        qkv.za_relay(-1, 3, 1)
        out.yb_relay(-3, 1)
        out.yb_relay(-3, -1)
        out.yb_own(4)
        qkv.fin(2)
        qkv.fin(-3)
        project((2, -3), False)
        out.yb_relay(3, 1)
        out.yb_relay(3, -1)
        out.za_relay(1, 3, 0)
        out.za_relay(-1, 3, 1)
        out.yb_relay(4, 1)
        out.yb_relay(4, -1)
        qkv.fin(3)
        qkv.fin(4)
        project((3, 4), False)
        whole[3].wait()
        whole[4].wait()
        attend(0, 1)
        attend(1, 1)
        attend(2, 1)
        attend(3, 1)
        attend(4, 1)
        attend(5, 1)
        out.fin(0)
        out.fin(-1)
        out.fin(1)
        out.fin(-2)
        out.fin(2)
        out.fin(-3)
        out.fin(3)
        out.fin(4)
        reduce_and_finish()
        for copy in links.started:
            copy.wait_send()


def shards(
    hidden_in, patch_ends, timestep, mod_weight, qkv_weight, out_weight, stale_keys, stale_values
):
    feats = jnp.broadcast_to(embed_time(timestep), (16, FREQ))
    marks = jnp.broadcast_to(jnp.pad(patch_ends, ((0, 0), (0, HD - patch_ends.shape[1]))), (8, HD))
    mod_mat = jnp.swapaxes(mod_weight[0], 0, 1)
    qkv_mat = jnp.swapaxes(qkv_weight[0], 0, 1)
    out_mat = jnp.swapaxes(out_weight[0], 0, 1)
    anywhere = pl.BlockSpec(memory_space=pl.ANY)
    vmem = pl.BlockSpec(memory_space=pltpu.VMEM)
    half = CW // 2
    result = pl.pallas_call(
        kernel,
        out_shape=jax.ShapeDtypeStruct((SLOT, CW), BF16),
        in_specs=[pl.BlockSpec(memory_space=pltpu.SMEM), vmem, vmem] + [anywhere] * 6,
        out_specs=vmem,
        scratch_shapes=[
            pltpu.VMEM((3, NZ, NY, KB, CW), BF16),
            pltpu.VMEM((NZ, NY, KB, OA), BF16),
            pltpu.VMEM((NZ, NY, KB, OB), BF16),
            pltpu.VMEM((3, FREQ, NX * CW), BF16),
            pltpu.VMEM((2, 3, 16, NX * CW), F32),
            pltpu.VMEM((2, NX, SLOT, CW), BF16),
            pltpu.VMEM((NZ, 2 * SLOT, SUP), BF16),
            pltpu.VMEM((3, SLOT, CW), F32),
            pltpu.VMEM((3, 2 * SLOT, half), F32),
            pltpu.VMEM((SLOT, CW), BF16),
            pltpu.VMEM((SLOT, CW), BF16),
            pltpu.VMEM((2, SLOT, half), BF16),
            pltpu.VMEM((2, SLOT, half), BF16),
            pltpu.VMEM((SLOT, CW), BF16),
            pltpu.VMEM((2 * SLOT, half), BF16),
            pltpu.VMEM((NX, 2 * SLOT, CW), BF16),
            pltpu.VMEM((2 * SLOT, CW), F32),
            pltpu.VMEM((3, 2 * SLOT, CW), BF16),
            pltpu.VMEM((SLOT, CW), BF16),
            pltpu.VMEM((16, FREQ), BF16),
            pltpu.VMEM((2, 8, HD), jnp.int32),
            pltpu.VMEM((SLOT, CW), BF16),
            pltpu.SemaphoreType.DMA((N_SEM,)),
            pltpu.SemaphoreType.DMA((N_SEM,)),
            pltpu.SemaphoreType.DMA((8,)),
            pltpu.SemaphoreType.DMA((2,)),
            pltpu.SemaphoreType.REGULAR,
        ],
        compiler_params=pltpu.CompilerParams(
            collective_id=0, has_side_effects=True, vmem_limit_bytes=62 * 1024 * 1024
        ),
        name="patch_layers",
    )(
        patch_ends, feats, marks, hidden_in[0], mod_mat, qkv_mat, out_mat,
        stale_keys[0, 0], stale_values[0, 0],
    )
    return result[None, None]


def solution(mesh):
    return jax.shard_map(
        shards,
        mesh=mesh,
        in_specs=(
            P("row", None, "col"),
            P("row", None),
            P("row"),
            P("section", None, None, None),
            P("section", "row", None, "col"),
            P("section", "col", "row"),
            P("section", "row", None, "col"),
            P("section", "row", None, "col"),
        ),
        out_specs=P("section", "row", None, "col"),
        check_vma=False,
    )
```
